512 devices in a mesh: field: 16 (over y_hi, x, core), space: 32 (over y_lo, z).
Axes of the slice: x: 4, y: 4 (y_hi: 2, y_lo: 2; y = y_hi * 2 + y_lo), z: 16, core: 2. Of those that a mesh axis runs over, the one named last changes fastest.
Arguments:
- scalars: float32 [16, 32, 64, 16, 128], P('field', None, 'space'), may hold values from 0.02 to 1
- diffusivity: float32 [64, 16, 128], P('space'), may hold values from 0.02 to 0.1
- velocity: float32 [64, 16, 128], P('space'), may hold values from 0 to 0.35
- mixing: float32 [64, 16, 128], P('space'), may hold values from 0.1 to 0.6
- rates: float32 [256], replicated, may hold values from 0.05 to 2
- stoich: int32 [4, 256], replicated, may hold values from 0 to 31
- burn_tile: int32 [16, 32, 32], P('field'), may hold values from -1 to 31, as said below
- helper_slot: int32 [16, 32, 32], P('field'), may hold values from -1 to 127, as said below
Outputs:
- updated: float32 [16, 32, 64, 16, 128], P('field', None, 'space')
The draws below stay inside these ranges and needn't reach their ends.
Inputs may be any that keep to these rules, and one draw needn't show every extreme that they name: Entries of burn_tile for one field and block are distinct tile numbers 0 to 31, live ones first and -1 after; one block lists at most 32, and some block of every field lists exactly 32. helper_slot is -1 exactly where burn_tile is -1; a live entry's slot h * 4 + p names helper block h and place p. In every field each slot 0 to 127 is used by exactly one live entry. The number of tiles that one block sends to one helper is at most 1, and equals 1 for some pair in every field.
All inputs are finite; a program needn't handle non-finite values.
Results may differ from the reference program's by a relative error of at most 0.0003.
Values sent between devices are 32-bit elements; how exact they have to be, the bound alone decides.
No kernel may reach another device: no remote copies, remote signals or barrier semaphores. Data moves between devices by JAX's collectives and lax.ppermute only.
A program may use at most 64 MiB of HBM per device.

```python
import math
import jax
import jax.numpy as jnp
from jax import lax

S = 32
R = 256
NX = 128
NY = 16
CZ = 2
NSUB = 4
MAXB = 32
HCAP = 4
FIELDS = 16
BLOCKS = 32
NZ = 64
TILES_DEV = 32


def burning_plan(key):
    base_key = jax.random.fold_in(key, 4242)
    total_slots = BLOCKS * HCAP
    spread = total_slots - MAXB

    def tile_choice(tile_key):
        return jax.random.permutation(tile_key, TILES_DEV)[:MAXB].astype(jnp.int32)

    def one_field(field_key):
        keys = jax.random.split(field_key, 4)
        order = jax.random.permutation(keys[0], BLOCKS)
        ranked = jnp.arange(BLOCKS, dtype=jnp.int32)
        share = spread // (BLOCKS - 1)
        extra = spread % (BLOCKS - 1)
        sorted_counts = jnp.where(ranked == 0, MAXB, share + (ranked <= extra).astype(jnp.int32)).astype(jnp.int32)
        counts = jnp.zeros((BLOCKS,), jnp.int32).at[order].set(sorted_counts)
        starts = jnp.cumsum(counts) - counts
        offset = jax.random.randint(keys[1], (), 0, total_slots)
        position = jnp.arange(MAXB, dtype=jnp.int32)[None, :]
        entry = (starts[:, None] + position + offset) % total_slots
        helpers = jax.random.permutation(keys[2], BLOCKS).astype(jnp.int32)
        slot = helpers[entry % BLOCKS] * HCAP + entry // BLOCKS
        live = position < counts[:, None]
        chosen = jax.vmap(tile_choice)(jax.random.split(keys[3], BLOCKS))
        return (jnp.where(live, chosen, -1).astype(jnp.int32), jnp.where(live, slot, -1).astype(jnp.int32))
    return jax.vmap(one_field)(jax.random.split(base_key, FIELDS))


def draw_burn_tile(key, part):
    return burning_plan(key)[0]


def draw_helper_slot(key, part):
    return burning_plan(key)[1]


def with_ends(values, key, smallest, top_value):
    place = [jax.random.randint(jax.random.fold_in(key, axis), (), 0, length) for axis, length in enumerate(values.shape)]
    widest = values.shape.index(max(values.shape))
    next_to = place[:widest] + [(place[widest] + 1) % values.shape[widest]] + place[widest + 1:]
    return values.at[tuple(place)].set(smallest).at[tuple(next_to)].set(top_value)


def levels(rng, shape, pieces, smallest, largest):
    level, own = 1.0, jax.random.fold_in(rng, 6)
    for dim, blocks in pieces:
        steps = jnp.exp(jax.random.uniform(jax.random.fold_in(own, dim), (blocks,), jnp.float32, smallest / len(pieces), largest / len(pieces)))
        level = level * jnp.repeat(steps, shape[dim] // blocks).reshape([-1 if axis == dim else 1 for axis in range(len(shape))])
    return level


def setup_inputs(seed: int = 0) -> dict:
    key_of = jax.random.split(jax.random.key(seed), 9)
    return {
        "scalars": jnp.clip(jnp.exp(math.log(1.0) - 3.912023 * jax.random.uniform(key_of[0], (FIELDS, S, NZ, NY, NX), jnp.float32) ** levels(key_of[0], (FIELDS, S, NZ, NY, NX), ((0, 16), (2, 32)), -0.2, 0.2)), 0.02, 1.0),
        "diffusivity": jnp.clip(jnp.exp(math.log(0.1) - 1.609438 * jax.random.uniform(key_of[1], (NZ, NY, NX), jnp.float32) ** levels(key_of[1], (NZ, NY, NX), ((0, 32),), -0.2, 0.2)), 0.02, 0.1),
        "velocity": jnp.clip(0.35 * jax.random.uniform(key_of[2], (NZ, NY, NX), jnp.float32) ** levels(key_of[2], (NZ, NY, NX), ((0, 32),), -0.2, 0.2), 0.0, 0.35),
        "mixing": jnp.clip(jnp.exp(math.log(0.6) - 1.7917595 * jax.random.uniform(key_of[3], (NZ, NY, NX), jnp.float32) ** levels(key_of[3], (NZ, NY, NX), ((0, 32),), -0.2, 0.2)), 0.1, 0.6),
        "rates": jnp.clip(jnp.exp(jax.random.uniform(key_of[4], (R,), jnp.float32, math.log(0.05), math.log(2.0))), 0.05, 2.0),
        "stoich": with_ends(jax.random.randint(key_of[5], (4, R), 0, S), jax.random.fold_in(key_of[5], 1), 0, S - 1).astype(jnp.int32),
        "burn_tile": draw_burn_tile(jax.random.fold_in(key_of[8], 71), 0),
        "helper_slot": draw_helper_slot(jax.random.fold_in(key_of[8], 71), 0),
    }


def transport(padded, diffusivity, velocity):
    center = padded[..., 1:-1, :, :]
    above_cells = padded[..., 2:, :, :]
    below_cells = padded[..., :-2, :, :]
    lateral = jnp.roll(center, 1, -1) + jnp.roll(center, -1, -1) + jnp.roll(center, 1, -2) + jnp.roll(center, -1, -2)
    return center + diffusivity * (above_cells + below_cells + lateral - 6.0 * center) + velocity * (below_cells - center)


def one_hot_rows(indices, count):
    return (indices[:, None] == jnp.arange(count, dtype=jnp.int32)[None, :]).astype(jnp.float32)


def reaction_tables(stoich, species):
    produced = one_hot_rows(stoich[2], species) + one_hot_rows(stoich[3], species)
    return one_hot_rows(stoich[0], species), one_hot_rows(stoich[1], species), produced


def chemistry(concent, tables, rates):
    reactant_one, reactant_two, produced = tables
    rate_col = rates[None, :, None]
    substep = 1.0 / NSUB
    highest = lax.Precision.HIGHEST
    for repeat in range(NSUB):
        conc_one = jnp.einsum("rs,nsc->nrc", reactant_one, concent, precision=highest)
        conc_two = jnp.einsum("rs,nsc->nrc", reactant_two, concent, precision=highest)
        progress = rate_col * conc_one * conc_two
        making = jnp.einsum("rs,nrc->nsc", produced, progress, precision=highest)
        losing = jnp.einsum("rs,nrc->nsc", reactant_one, rate_col * conc_two, precision=highest)
        losing = losing + jnp.einsum("rs,nrc->nsc", reactant_two, rate_col * conc_one, precision=highest)
        concent = (concent + substep * making) / (1.0 + substep * losing)
    return concent


def reference(scalars, diffusivity, velocity, mixing, rates, stoich, burn_tile, helper_slot):
    padded = jnp.concatenate([scalars[:, :, -1:], scalars, scalars[:, :, :1]], axis=2)
    advected = transport(padded, diffusivity, velocity)
    ensemble = jnp.sum(advected, axis=0) / FIELDS
    mixed = advected - mixing * (advected - ensemble)
    species = mixed.shape[1]
    tables = reaction_tables(stoich, species)
    tiles_dev = CZ * NY
    all_tiles = NZ * NY
    slot_iota = jnp.arange(BLOCKS * HCAP, dtype=jnp.int32)
    block_base = (jnp.arange(BLOCKS, dtype=jnp.int32) * tiles_dev)[:, None]

    def one_field(inputs):
        field_rows, tile_list, slot_list = inputs
        tile_grid = field_rows.reshape(species, all_tiles, NX)
        global_tile = jnp.where(tile_list >= 0, block_base + tile_list, 0).reshape(-1).astype(jnp.int32)
        matches = slot_list.reshape(-1)[None, :] == slot_iota[:, None]
        slot_tile = jnp.sum(jnp.where(matches, global_tile[None, :], 0), axis=1).astype(jnp.int32)
        burning = jnp.transpose(tile_grid[:, slot_tile, :], (1, 0, 2))
        reacted = chemistry(burning, tables, rates)
        tile_grid = tile_grid.at[:, slot_tile, :].set(jnp.transpose(reacted, (1, 0, 2)))
        return tile_grid.reshape(field_rows.shape)

    return lax.map(one_field, (mixed, burn_tile, helper_slot))
```

```python
import functools

import jax
import jax.numpy as jnp
from jax import lax
from jax.experimental import pallas as pl
from jax.experimental.pallas import tpu as pltpu
from jax.sharding import PartitionSpec as P

NSUB = 4
LANES = 128
GROUP = 8
F32 = jnp.float32
BF16 = jnp.bfloat16
VMEM = pl.BlockSpec(memory_space=pltpu.VMEM)
SMEM = pl.BlockSpec(memory_space=pltpu.SMEM)
LIMIT = pltpu.CompilerParams(vmem_limit_bytes=24 << 20)


def shape(*dims):
    return jax.ShapeDtypeStruct(dims, F32)


def transport_kernel(parity_ref, tiles_ref, cells_ref, near_ref, far_ref, dif_ref, vel_ref, out_ref, rows_ref):
    species, planes, rows, _ = cells_ref.shape
    odd = parity_ref[0] == 1
    dif = [dif_ref[z] for z in range(planes)]
    vel = [vel_ref[z] for z in range(planes)]

    def one_species(s, carry):
        near, far = near_ref[s, 0], far_ref[s, 0]
        below = jnp.where(odd, near, far)
        above = jnp.where(odd, far, near)
        cells = [cells_ref[s, z] for z in range(planes)]
        column = [below, *cells, above]
        for z in range(planes):
            center, under, over = column[z + 1], column[z], column[z + 2]
            lateral = (
                pltpu.roll(center, 1, 1)
                + pltpu.roll(center, LANES - 1, 1)
                + pltpu.roll(center, 1, 0)
                + pltpu.roll(center, rows - 1, 0)
            )
            moved = center + dif[z] * (over + under + lateral - 6.0 * center) + vel[z] * (under - center)
            start = pl.multiple_of((s * planes + z) * rows, rows)
            rows_ref[pl.ds(start, rows), :] = moved
        return carry

    lax.fori_loop(0, species, one_species, 0, unroll=4)
    data = species * planes
    for y in range(rows):
        out_ref[y, 0:data, :] = rows_ref[pl.ds(y, data, stride=rows), :]
        out_ref[y, data : data + 8, :] = jnp.zeros((8, LANES), F32)
    for entry in range(tiles_ref.shape[0]):
        tile = tiles_ref[entry]

        @pl.when(tile >= 0)
        def _():
            y, z = lax.rem(tile, rows), lax.div(tile, rows)
            out_ref[y, pl.ds(data + z, 1), :] = jnp.ones((1, LANES), F32)


def in_parts(x, count):
    parts = []
    for part in range(count):
        parts.append(x.astype(BF16))
        if part + 1 < count:
            x = x - parts[-1].astype(F32)
    return parts


def chemistry(concent, pick, partner, produced, rates):
    substep = 1.0 / NSUB
    reactions = rates.shape[0]
    for repeat in range(NSUB):
        high, low = in_parts(concent, 2)
        picked = jnp.dot(pick, jnp.concatenate([high, low], 0), preferred_element_type=F32)
        losing = jnp.dot(partner, jnp.concatenate([high, high, low], 0), preferred_element_type=F32)
        progress = picked[:reactions] * picked[reactions:] * rates
        high, low = in_parts(progress, 2)
        making = jnp.dot(produced, high, preferred_element_type=F32) + jnp.dot(
            produced, low, preferred_element_type=F32
        )
        concent = (concent + substep * making) / (1.0 + substep * losing)
    return concent


def react_kernel(row_ref, in_ref, mix_ref, pick_ref, partner_ref, produced_ref, rates_ref, out_ref, list_ref):
    fields, data, _ = out_ref.shape
    planes = mix_ref.shape[0]
    species = data // planes
    row = row_ref[0]
    even = lax.broadcasted_iota(jnp.int32, (8, LANES), 0) % planes == 0
    mixing = jnp.where(even, mix_ref[0, pl.ds(row, 1), :], mix_ref[1, pl.ds(row, 1), :])

    def one_block(block, carry):
        at = pl.ds(pl.multiple_of(block * 8, 8), 8)
        cells = [in_ref[f, at, :] for f in range(fields)]
        total = cells[0]
        for f in range(1, fields):
            total = total + cells[f]
        ensemble = total * (1.0 / fields)
        for f in range(fields):
            out_ref[f, at, :] = cells[f] - mixing * (cells[f] - ensemble)
        return carry

    lax.fori_loop(0, data // 8, one_block, 0)
    marks = jnp.zeros((8, LANES), F32)
    for f in range(fields):
        marks = marks + in_ref[f, data : data + 8, :] * float(2**f)
    code = [jnp.max(marks[z : z + 1, :]).astype(jnp.int32) for z in range(planes)]
    count = jnp.int32(0)
    for z in range(planes):
        for f in range(fields):
            list_ref[count] = f * planes + z
            count = count + ((code[z] >> f) & 1)
    rates = jnp.concatenate([rates_ref[...]] * GROUP, 1)
    pick, partner, produced = pick_ref[...], partner_ref[...], produced_ref[...]

    @pl.loop(0, pl.cdiv(count, GROUP))
    def _(group):
        first = group * GROUP
        entries = [list_ref[jnp.minimum(first + j, count - 1)] for j in range(GROUP)]
        places = [(lax.div(e, planes), lax.rem(e, planes)) for e in entries]
        concent = jnp.concatenate([out_ref[f, pl.ds(z, species, stride=planes), :] for f, z in places], 1)
        concent = chemistry(concent, pick, partner, produced, rates)
        for j, (f, z) in enumerate(places):

            @pl.when(first + j < count)
            def _():
                out_ref[f, pl.ds(z, species, stride=planes), :] = concent[:, j * LANES : (j + 1) * LANES]


def home_kernel(in_ref, out_ref, rows_ref):
    pieces, data, _ = in_ref.shape
    for y in range(pieces):
        rows_ref[pl.ds(y, data, stride=pieces), :] = in_ref[y]
    out_ref[...] = rows_ref[...].reshape(out_ref.shape)


def one_hot_rows(indices, count):
    return (indices[:, None] == jnp.arange(count, dtype=jnp.int32)[None, :]).astype(F32)


def reaction_tables(stoich, rates, species):
    one, two = one_hot_rows(stoich[0], species), one_hot_rows(stoich[1], species)
    produced = one_hot_rows(stoich[2], species) + one_hot_rows(stoich[3], species)
    pick = jnp.concatenate([one, two], 0).astype(BF16)
    partner = jnp.dot((one * rates[:, None]).T, two, precision=lax.Precision.HIGHEST)
    partner = partner + partner.T
    high = lax.reduce_precision(partner, 8, 7)
    low = partner - high
    return (
        jnp.concatenate([pick, pick], 1),
        jnp.concatenate([high, low, high], 1).astype(BF16),
        produced.T.astype(BF16),
        jnp.broadcast_to(rates[:, None], (rates.shape[0], LANES)),
    )


def per_device(scalars, diffusivity, velocity, mixing, rates, stoich, burn_tile, helper_slot):
    block = lax.axis_index("space")
    blocks = lax.axis_size("space")
    fields = lax.axis_size("field")
    cells = scalars[0]
    species, planes, rows, width = cells.shape
    data = species * planes
    parity = block % 2
    near_pairs = [(i, i ^ 1) for i in range(blocks)]
    far_pairs = [(i, (i + 1 if i % 2 else i - 1) % blocks) for i in range(blocks)]
    far = lax.ppermute(lax.dynamic_slice_in_dim(cells, parity, 1, 1), "space", far_pairs)
    near = lax.ppermute(lax.dynamic_slice_in_dim(cells, 1 - parity, 1, 1), "space", near_pairs)
    tables = reaction_tables(stoich, rates, species)
    pieces = pl.pallas_call(
        transport_kernel,
        out_shape=shape(rows, data + 8, width),
        in_specs=[SMEM, SMEM] + [VMEM] * 5,
        out_specs=VMEM,
        scratch_shapes=[pltpu.VMEM((data * rows, width), F32)],
        compiler_params=LIMIT,
        name="transport",
    )(parity.reshape(1), burn_tile[0, block], cells, near, far, diffusivity, velocity)
    pieces = lax.all_to_all(pieces, "field", 0, 0, tiled=True)
    pieces = pl.pallas_call(
        react_kernel,
        out_shape=shape(fields, data, width),
        in_specs=[SMEM] + [VMEM] * 6,
        out_specs=VMEM,
        scratch_shapes=[pltpu.SMEM((fields * planes + 1,), jnp.int32)],
        compiler_params=LIMIT,
        name="react",
    )(lax.axis_index("field").reshape(1), pieces, mixing, *tables)
    pieces = lax.all_to_all(pieces, "field", 0, 0, tiled=True)
    updated = pl.pallas_call(
        home_kernel,
        out_shape=shape(species, planes, rows, width),
        in_specs=[VMEM],
        out_specs=VMEM,
        scratch_shapes=[pltpu.VMEM((data * rows, width), F32)],
        compiler_params=LIMIT,
        name="home",
    )(pieces)
    return updated[None]


def solution(mesh):
    return jax.shard_map(
        per_device,
        mesh=mesh,
        in_specs=(
            P("field", None, "space", None, None),
            P("space", None, None),
            P("space", None, None),
            P("space", None, None),
            P(),
            P(),
            P("field", None, None),
            P("field", None, None),
        ),
        out_specs=P("field", None, "space", None, None),
        check_vma=False,
    )
```

```python
import functools

import jax
import jax.numpy as jnp
from jax import lax
from jax.experimental import pallas as pl
from jax.experimental.pallas import tpu as pltpu
from jax.sharding import PartitionSpec as P

NSUB = 4
LANES = 128
GROUP = 8
F32 = jnp.float32
BF16 = jnp.bfloat16
VMEM = pl.BlockSpec(memory_space=pltpu.VMEM)
SMEM = pl.BlockSpec(memory_space=pltpu.SMEM)
LIMIT = pltpu.CompilerParams(vmem_limit_bytes=24 << 20)


def shape(*dims):
    return jax.ShapeDtypeStruct(dims, F32)


def plane_kernel(plane, cells_ref, out_ref, sem):
    copy = pltpu.make_async_copy(cells_ref.at[:, plane], out_ref, sem)
    copy.start()
    copy.wait()


def plane_of(cells, plane):
    species, _, rows, width = cells.shape
    return pl.pallas_call(
        functools.partial(plane_kernel, plane),
        out_shape=shape(species, rows, width),
        in_specs=[pl.BlockSpec(memory_space=pltpu.HBM)],
        out_specs=VMEM,
        scratch_shapes=[pltpu.SemaphoreType.DMA],
        compiler_params=LIMIT,
        name="plane",
    )(pltpu.with_memory_space_constraint(cells, pltpu.HBM))


def local_kernel(tiles_ref, cells_ref, dif_ref, vel_ref, out_ref, rows_ref):
    species, planes, rows, _ = cells_ref.shape
    last = planes - 1
    dif = [dif_ref[z] for z in range(planes)]
    vel = [vel_ref[z] for z in range(planes)]

    def one_species(s, carry):
        cells = [cells_ref[s, z] for z in range(planes)]
        for z in range(planes):
            center = cells[z]
            around = (
                pltpu.roll(center, 1, 1)
                + pltpu.roll(center, LANES - 1, 1)
                + pltpu.roll(center, 1, 0)
                + pltpu.roll(center, rows - 1, 0)
                - 6.0 * center
            )
            if z > 0:
                around = around + cells[z - 1]
            if z < last:
                around = around + cells[z + 1]
            drift = cells[z - 1] - center if z > 0 else -center
            start = pl.multiple_of((s * planes + z) * rows, rows)
            rows_ref[pl.ds(start, rows), :] = center + dif[z] * around + vel[z] * drift
        return carry

    lax.fori_loop(0, species, one_species, 0, unroll=4)
    data = species * planes
    for y in range(rows):
        out_ref[y, 0:data, :] = rows_ref[pl.ds(y, data, stride=rows), :]
        out_ref[y, data : data + 8, :] = jnp.zeros((8, LANES), F32)
    for entry in range(tiles_ref.shape[0]):
        tile = tiles_ref[entry]

        @pl.when(tile >= 0)
        def _():
            y, z = lax.rem(tile, rows), lax.div(tile, rows)
            out_ref[y, pl.ds(data + z, 1), :] = jnp.ones((1, LANES), F32)


def halo_kernel(pieces_ref, below_ref, above_ref, dif_ref, vel_ref, out_ref):
    planes, rows, _ = dif_ref.shape
    species = below_ref.shape[0] // rows
    for y in range(rows):
        at = pl.ds(y, species, stride=rows)
        low = dif_ref[0, y : y + 1, :] + vel_ref[0, y : y + 1, :]
        high = dif_ref[planes - 1, y : y + 1, :]
        first, last = pl.ds(0, species, stride=planes), pl.ds(planes - 1, species, stride=planes)
        out_ref[y, first, :] = pieces_ref[y, first, :] + low * below_ref[at, :]
        out_ref[y, last, :] = pieces_ref[y, last, :] + high * above_ref[at, :]


def in_parts(x, count):
    parts = []
    for part in range(count):
        parts.append(x.astype(BF16))
        if part + 1 < count:
            x = x - parts[-1].astype(F32)
    return parts


def chemistry(concent, pick, partner, produced, rates):
    substep = 1.0 / NSUB
    reactions = rates.shape[0]
    for repeat in range(NSUB):
        high, low = in_parts(concent, 2)
        picked = jnp.dot(pick, jnp.concatenate([high, low], 0), preferred_element_type=F32)
        losing = jnp.dot(partner, jnp.concatenate([high, high, low], 0), preferred_element_type=F32)
        progress = picked[:reactions] * picked[reactions:] * rates
        high, low = in_parts(progress, 2)
        making = jnp.dot(produced, high, preferred_element_type=F32) + jnp.dot(
            produced, low, preferred_element_type=F32
        )
        concent = (concent + substep * making) / (1.0 + substep * losing)
    return concent


def react_kernel(in_ref, mix_ref, pick_ref, partner_ref, produced_ref, rates_ref, out_ref, list_ref):
    fields, data, _ = out_ref.shape
    planes = mix_ref.shape[0]
    species = data // planes
    even = lax.broadcasted_iota(jnp.int32, (8, LANES), 0) % planes == 0
    mixing = jnp.where(even, mix_ref[0:1, :], mix_ref[1:2, :])

    def one_block(block, carry):
        at = pl.ds(pl.multiple_of(block * 8, 8), 8)
        cells = [in_ref[f, at, :] for f in range(fields)]
        total = cells[0]
        for f in range(1, fields):
            total = total + cells[f]
        ensemble = total * (1.0 / fields)
        for f in range(fields):
            out_ref[f, at, :] = cells[f] - mixing * (cells[f] - ensemble)
        return carry

    lax.fori_loop(0, data // 8, one_block, 0)
    marks = jnp.zeros((8, LANES), F32)
    for f in range(fields):
        marks = marks + in_ref[f, data : data + 8, :] * float(2**f)
    code = [jnp.max(marks[z : z + 1, :]).astype(jnp.int32) for z in range(planes)]
    count = jnp.int32(0)
    for z in range(planes):
        for f in range(fields):
            list_ref[count] = f * planes + z
            count = count + ((code[z] >> f) & 1)
    rates = jnp.concatenate([rates_ref[...]] * GROUP, 1)
    pick, partner, produced = pick_ref[...], partner_ref[...], produced_ref[...]

    @pl.loop(0, pl.cdiv(count, GROUP))
    def _(group):
        first = group * GROUP
        entries = [list_ref[jnp.minimum(first + j, count - 1)] for j in range(GROUP)]
        places = [(lax.div(e, planes), lax.rem(e, planes)) for e in entries]
        concent = jnp.concatenate([out_ref[f, pl.ds(z, species, stride=planes), :] for f, z in places], 1)
        concent = chemistry(concent, pick, partner, produced, rates)
        for j, (f, z) in enumerate(places):

            @pl.when(first + j < count)
            def _():
                out_ref[f, pl.ds(z, species, stride=planes), :] = concent[:, j * LANES : (j + 1) * LANES]


def home_kernel(in_ref, out_ref):
    pieces, data, _ = in_ref.shape
    for y in range(pieces):
        out_ref[pl.ds(y, data, stride=pieces), :] = in_ref[y]


def one_hot_rows(indices, count):
    return (indices[:, None] == jnp.arange(count, dtype=jnp.int32)[None, :]).astype(F32)


def reaction_tables(stoich, rates, species):
    one, two = one_hot_rows(stoich[0], species), one_hot_rows(stoich[1], species)
    produced = one_hot_rows(stoich[2], species) + one_hot_rows(stoich[3], species)
    pick = jnp.concatenate([one, two], 0).astype(BF16)
    partner = jnp.dot((one * rates[:, None]).T, two, precision=lax.Precision.HIGHEST)
    partner = partner + partner.T
    high = lax.reduce_precision(partner, 8, 7)
    low = partner - high
    return (
        jnp.concatenate([pick, pick], 1),
        jnp.concatenate([high, low, high], 1).astype(BF16),
        produced.T.astype(BF16),
        jnp.broadcast_to(rates[:, None], (rates.shape[0], LANES)),
    )


def per_device(scalars, diffusivity, velocity, mixing, rates, stoich, burn_tile, helper_slot):
    block = lax.axis_index("space")
    blocks = lax.axis_size("space")
    fields = lax.axis_size("field")
    cells = scalars[0]
    species, planes, rows, width = cells.shape
    data = species * planes
    up = [(i, (i + 1) % blocks) for i in range(blocks)]
    down = [((i + 1) % blocks, i) for i in range(blocks)]
    below = lax.ppermute(plane_of(cells, planes - 1), "space", up).reshape(species * rows, width)
    above = lax.ppermute(plane_of(cells, 0), "space", down).reshape(species * rows, width)
    tables = reaction_tables(stoich, rates, species)
    mixing_row = lax.dynamic_index_in_dim(mixing, lax.axis_index("field"), 1, False)
    pieces = pl.pallas_call(
        local_kernel,
        out_shape=shape(rows, data + 8, width),
        in_specs=[SMEM] + [VMEM] * 3,
        out_specs=VMEM,
        scratch_shapes=[pltpu.VMEM((data * rows, width), F32)],
        compiler_params=LIMIT,
        name="local",
    )(burn_tile[0, block], cells, diffusivity, velocity)
    pieces = pl.pallas_call(
        halo_kernel,
        out_shape=shape(rows, data + 8, width),
        in_specs=[VMEM] * 5,
        out_specs=VMEM,
        input_output_aliases={0: 0},
        compiler_params=LIMIT,
        name="halo",
    )(pieces, below, above, diffusivity, velocity)
    pieces, tables, mixing_row = lax.optimization_barrier((pieces, tables, mixing_row))
    pieces = lax.all_to_all(pieces, "field", 0, 0, tiled=True)
    pieces = pl.pallas_call(
        react_kernel,
        out_shape=shape(fields, data, width),
        in_specs=[VMEM] * 6,
        out_specs=VMEM,
        scratch_shapes=[pltpu.SMEM((fields * planes + 1,), jnp.int32)],
        compiler_params=LIMIT,
        name="react",
    )(pieces, mixing_row, *tables)
    pieces = lax.all_to_all(pieces, "field", 0, 0, tiled=True)
    steps = 4
    updated = pl.pallas_call(
        home_kernel,
        grid=(steps,),
        out_shape=shape(data * rows, width),
        in_specs=[pl.BlockSpec((rows, data // steps, width), lambda i: (0, i, 0))],
        out_specs=pl.BlockSpec((data * rows // steps, width), lambda i: (i, 0)),
        compiler_params=LIMIT,
        name="home",
    )(pieces)
    return updated.reshape(1, species, planes, rows, width)


def solution(mesh):
    return jax.shard_map(
        per_device,
        mesh=mesh,
        in_specs=(
            P("field", None, "space", None, None),
            P("space", None, None),
            P("space", None, None),
            P("space", None, None),
            P(),
            P(),
            P("field", None, None),
            P("field", None, None),
        ),
        out_specs=P("field", None, "space", None, None),
        check_vma=False,
    )
```

```python
import functools

import jax
import jax.numpy as jnp
from jax import lax
from jax.experimental import pallas as pl
from jax.experimental.pallas import tpu as pltpu
from jax.sharding import PartitionSpec as P

NSUB = 4
LANES = 128
GROUP = 12
F32 = jnp.float32
BF16 = jnp.bfloat16
VMEM = pl.BlockSpec(memory_space=pltpu.VMEM)
SMEM = pl.BlockSpec(memory_space=pltpu.SMEM)
LIMIT = pltpu.CompilerParams(vmem_limit_bytes=24 << 20)


def shape(*dims):
    return jax.ShapeDtypeStruct(dims, F32)


def local_kernel(tiles_ref, cells_ref, dif_ref, vel_ref, out_ref, rows_ref):
    species, planes, rows, _ = cells_ref.shape
    last = planes - 1
    dif = [dif_ref[z] for z in range(planes)]
    vel = [vel_ref[z] for z in range(planes)]

    def one_species(s, carry):
        cells = [cells_ref[s, z] for z in range(planes)]
        for z in range(planes):
            center = cells[z]
            around = (
                pltpu.roll(center, 1, 1)
                + pltpu.roll(center, LANES - 1, 1)
                + pltpu.roll(center, 1, 0)
                + pltpu.roll(center, rows - 1, 0)
                - 6.0 * center
            )
            if z > 0:
                around = around + cells[z - 1]
            if z < last:
                around = around + cells[z + 1]
            drift = cells[z - 1] - center if z > 0 else -center
            start = pl.multiple_of((s * planes + z) * rows, rows)
            rows_ref[pl.ds(start, rows), :] = center + dif[z] * around + vel[z] * drift
        return carry

    lax.fori_loop(0, species, one_species, 0, unroll=4)
    data = species * planes
    for y in range(rows):
        out_ref[y, 0:data, :] = rows_ref[pl.ds(y, data, stride=rows), :]
        out_ref[y, data : data + 8, :] = jnp.zeros((8, LANES), F32)
    for entry in range(tiles_ref.shape[0]):
        tile = tiles_ref[entry]

        @pl.when(tile >= 0)
        def _():
            y, z = lax.rem(tile, rows), lax.div(tile, rows)
            out_ref[y, pl.ds(data + z, 1), :] = jnp.ones((1, LANES), F32)


def halo_kernel(pieces_ref, below_ref, above_ref, dif_ref, vel_ref, out_ref):
    planes, rows, _ = dif_ref.shape
    species = below_ref.shape[0] // rows
    for y in range(rows):
        at = pl.ds(y, species, stride=rows)
        low = dif_ref[0, y : y + 1, :] + vel_ref[0, y : y + 1, :]
        high = dif_ref[planes - 1, y : y + 1, :]
        first, last = pl.ds(0, species, stride=planes), pl.ds(planes - 1, species, stride=planes)
        out_ref[y, first, :] = pieces_ref[y, first, :] + low * below_ref[at, :]
        out_ref[y, last, :] = pieces_ref[y, last, :] + high * above_ref[at, :]


def in_parts(x):
    high = x.astype(BF16)
    return high, (x - high.astype(F32)).astype(BF16)


def factors(x):
    high, low = in_parts(x)
    return jnp.concatenate([high, low, high], 0)


def weights(w):
    high = lax.reduce_precision(w, 8, 7)
    return jnp.concatenate([high, high, w - high], 1).astype(BF16)


def dot(a, b):
    return jnp.dot(a, b, preferred_element_type=F32)


def chemistry(concent, pairs, partner, squares, produced):
    substep = 1.0 / NSUB
    for repeat in range(NSUB):
        current = factors(concent)
        pair = dot(pairs, current)
        making = dot(produced, jnp.concatenate(in_parts(pair * pair), 0)) - dot(squares, factors(concent * concent))
        concent = (concent + substep * making) / (1.0 + substep * dot(partner, current))
    return concent


def react_kernel(in_ref, mix_ref, pairs_ref, partner_ref, squares_ref, produced_ref, out_ref, list_ref):
    fields, data, _ = out_ref.shape
    planes = mix_ref.shape[0]
    species = data // planes
    even = lax.broadcasted_iota(jnp.int32, (8, LANES), 0) % planes == 0
    mixing = jnp.where(even, mix_ref[0:1, :], mix_ref[1:2, :])

    def one_block(block, carry):
        at = pl.ds(pl.multiple_of(block * 8, 8), 8)
        cells = [in_ref[f, at, :] for f in range(fields)]
        total = cells[0]
        for f in range(1, fields):
            total = total + cells[f]
        ensemble = total * (1.0 / fields)
        for f in range(fields):
            out_ref[f, at, :] = cells[f] - mixing * (cells[f] - ensemble)
        return carry

    lax.fori_loop(0, data // 8, one_block, 0)
    marks = jnp.zeros((8, LANES), F32)
    for f in range(fields):
        marks = marks + in_ref[f, data : data + 8, :] * float(2**f)
    code = [jnp.max(marks[z : z + 1, :]).astype(jnp.int32) for z in range(planes)]
    count = jnp.int32(0)
    for z in range(planes):
        for f in range(fields):
            list_ref[count] = f * planes + z
            count = count + ((code[z] >> f) & 1)
    tables = [ref[...] for ref in (pairs_ref, partner_ref, squares_ref, produced_ref)]

    @pl.loop(0, pl.cdiv(count, GROUP))
    def _(group):
        first = group * GROUP
        entries = [list_ref[jnp.minimum(first + j, count - 1)] for j in range(GROUP)]
        places = [(lax.div(e, planes), lax.rem(e, planes)) for e in entries]
        concent = jnp.concatenate([out_ref[f, pl.ds(z, species, stride=planes), :] for f, z in places], 1)
        concent = chemistry(concent, *tables)
        for j, (f, z) in enumerate(places):

            @pl.when(first + j < count)
            def _():
                out_ref[f, pl.ds(z, species, stride=planes), :] = concent[:, j * LANES : (j + 1) * LANES]


def home_kernel(in_ref, out_ref, rows_ref, sems):
    pieces, data, _ = in_ref.shape
    steps = sems.shape[0]
    part = data // steps
    copies = []
    for step in range(steps):
        size = part * pieces
        for y in range(pieces):
            at = pl.ds(step * size + y, part, stride=pieces)
            rows_ref[at, :] = in_ref[y, step * part : (step + 1) * part, :]
        at = pl.ds(step * size, size)
        copies.append(pltpu.make_async_copy(rows_ref.at[at], out_ref.at[at], sems.at[step]))
        copies[-1].start()
    for copy in copies:
        copy.wait()


def one_hot_rows(indices, count):
    return (indices[:, None] == jnp.arange(count, dtype=jnp.int32)[None, :]).astype(F32)


def reaction_tables(stoich, rates, species):
    highest = lax.Precision.HIGHEST
    rate = rates[:, None]
    one, two = one_hot_rows(stoich[0], species), one_hot_rows(stoich[1], species)
    produced = one_hot_rows(stoich[2], species) + one_hot_rows(stoich[3], species)
    both = one + two
    partner = jnp.dot((one * rate).T, two, precision=highest)
    squares = jnp.dot(produced.T, (0.5 * rate) * both, precision=highest)
    produced = (0.5 * produced).T.astype(BF16)
    return (
        weights(jnp.sqrt(rate) * both),
        weights(partner + partner.T),
        weights(squares),
        jnp.concatenate([produced, produced], 1),
    )


def per_device(scalars, diffusivity, velocity, mixing, rates, stoich, burn_tile, helper_slot):
    block = lax.axis_index("space")
    blocks = lax.axis_size("space")
    fields = lax.axis_size("field")
    cells = scalars[0]
    species, planes, rows, width = cells.shape
    data = species * planes
    up = [(i, (i + 1) % blocks) for i in range(blocks)]
    down = [((i + 1) % blocks, i) for i in range(blocks)]
    below = lax.ppermute(cells[:, planes - 1], "space", up).reshape(species * rows, width)
    above = lax.ppermute(cells[:, 0], "space", down).reshape(species * rows, width)
    tables = reaction_tables(stoich, rates, species)
    mixing_row = lax.dynamic_index_in_dim(mixing, lax.axis_index("field"), 1, False)
    pieces = pl.pallas_call(
        local_kernel,
        out_shape=shape(rows, data + 8, width),
        in_specs=[SMEM] + [VMEM] * 3,
        out_specs=VMEM,
        scratch_shapes=[pltpu.VMEM((data * rows, width), F32)],
        compiler_params=LIMIT,
        name="local",
    )(burn_tile[0, block], cells, diffusivity, velocity)
    pieces = pl.pallas_call(
        halo_kernel,
        out_shape=shape(rows, data + 8, width),
        in_specs=[VMEM] * 5,
        out_specs=VMEM,
        input_output_aliases={0: 0},
        compiler_params=LIMIT,
        name="halo",
    )(pieces, below, above, diffusivity, velocity)
    pieces, tables, mixing_row = lax.optimization_barrier((pieces, tables, mixing_row))
    pieces = lax.all_to_all(pieces, "field", 0, 0, tiled=True)
    pieces = pl.pallas_call(
        react_kernel,
        out_shape=shape(fields, data, width),
        in_specs=[VMEM] * 6,
        out_specs=VMEM,
        scratch_shapes=[pltpu.SMEM((fields * planes + 1,), jnp.int32)],
        compiler_params=LIMIT,
        name="react",
    )(pieces, mixing_row, *tables)
    pieces = lax.all_to_all(pieces, "field", 0, 0, tiled=True)
    updated = pl.pallas_call(
        home_kernel,
        out_shape=shape(data * rows, width),
        in_specs=[VMEM],
        out_specs=pl.BlockSpec(memory_space=pltpu.HBM),
        scratch_shapes=[pltpu.VMEM((data * rows, width), F32), pltpu.SemaphoreType.DMA((4,))],
        compiler_params=LIMIT,
        name="home",
    )(pieces)
    return updated.reshape(1, species, planes, rows, width)


def solution(mesh):
    return jax.shard_map(
        per_device,
        mesh=mesh,
        in_specs=(
            P("field", None, "space", None, None),
            P("space", None, None),
            P("space", None, None),
            P("space", None, None),
            P(),
            P(),
            P("field", None, None),
            P("field", None, None),
        ),
        out_specs=P("field", None, "space", None, None),
        check_vma=False,
    )
```

```python
import functools

import jax
import jax.numpy as jnp
from jax import lax
from jax.experimental import pallas as pl
from jax.experimental.pallas import tpu as pltpu
from jax.sharding import PartitionSpec as P

NSUB = 4
LANES = 128
GROUP = 12
F32 = jnp.float32
BF16 = jnp.bfloat16
VMEM = pl.BlockSpec(memory_space=pltpu.VMEM)
SMEM = pl.BlockSpec(memory_space=pltpu.SMEM)
LIMIT = pltpu.CompilerParams(vmem_limit_bytes=24 << 20)


def shape(*dims):
    return jax.ShapeDtypeStruct(dims, F32)


def local_kernel(tiles_ref, cells_ref, dif_ref, vel_ref, out_ref, rows_ref):
    species, planes, rows, _ = cells_ref.shape
    last = planes - 1
    dif = [dif_ref[z] for z in range(planes)]
    vel = [vel_ref[z] for z in range(planes)]

    def one_species(s, carry):
        cells = [cells_ref[s, z] for z in range(planes)]
        for z in range(planes):
            center = cells[z]
            around = (
                pltpu.roll(center, 1, 1)
                + pltpu.roll(center, LANES - 1, 1)
                + pltpu.roll(center, 1, 0)
                + pltpu.roll(center, rows - 1, 0)
                - 6.0 * center
            )
            if z > 0:
                around = around + cells[z - 1]
            if z < last:
                around = around + cells[z + 1]
            drift = cells[z - 1] - center if z > 0 else -center
            start = pl.multiple_of((s * planes + z) * rows, rows)
            rows_ref[pl.ds(start, rows), :] = center + dif[z] * around + vel[z] * drift
        return carry

    lax.fori_loop(0, species, one_species, 0, unroll=4)
    data = species * planes
    for y in range(rows):
        out_ref[y, 0:data, :] = rows_ref[pl.ds(y, data, stride=rows), :]
        out_ref[y, data : data + 8, :] = jnp.zeros((8, LANES), F32)
    for entry in range(tiles_ref.shape[0]):
        tile = tiles_ref[entry]

        @pl.when(tile >= 0)
        def _():
            y, z = lax.rem(tile, rows), lax.div(tile, rows)
            out_ref[y, pl.ds(data + z, 1), :] = jnp.ones((1, LANES), F32)


def halo_kernel(core_ref, pieces_ref, first_ref, second_ref, dif_ref, vel_ref, out_ref):
    planes, rows, _ = dif_ref.shape
    species = first_ref.shape[0] // rows
    low = dif_ref[0] + vel_ref[0]
    high = dif_ref[planes - 1]

    def add(below_ref, above_ref):
        for y in range(rows):
            at = pl.ds(y, species, stride=rows)
            bottom, top = pl.ds(0, species, stride=planes), pl.ds(planes - 1, species, stride=planes)
            out_ref[y, bottom, :] = pieces_ref[y, bottom, :] + low[y : y + 1] * below_ref[at, :]
            out_ref[y, top, :] = pieces_ref[y, top, :] + high[y : y + 1] * above_ref[at, :]

    @pl.when(core_ref[0] == 0)
    def _():
        add(first_ref, second_ref)

    @pl.when(core_ref[0] == 1)
    def _():
        add(second_ref, first_ref)


def in_parts(x):
    high = x.astype(BF16)
    return high, (x - high.astype(F32)).astype(BF16)


def factors(x):
    high, low = in_parts(x)
    return jnp.concatenate([high, low, high], 0)


def weights(w):
    high = lax.reduce_precision(w, 8, 7)
    return jnp.concatenate([high, high, w - high], 1).astype(BF16)


def dot(a, b):
    return jnp.dot(a, b, preferred_element_type=F32)


def chemistry(concent, pairs, partner, squares, produced):
    substep = 1.0 / NSUB
    for repeat in range(NSUB):
        current = factors(concent)
        pair = dot(pairs, current)
        making = dot(produced, jnp.concatenate(in_parts(pair * pair), 0)) - dot(squares, factors(concent * concent))
        concent = (concent + substep * making) / (1.0 + substep * dot(partner, current))
    return concent


def react_kernel(in_ref, mix_ref, pairs_ref, partner_ref, squares_ref, produced_ref, out_ref, list_ref):
    fields, data, _ = out_ref.shape
    planes = mix_ref.shape[0]
    species = data // planes
    even = lax.broadcasted_iota(jnp.int32, (8, LANES), 0) % planes == 0
    mixing = jnp.where(even, mix_ref[0:1, :], mix_ref[1:2, :])

    def one_block(block, carry):
        at = pl.ds(pl.multiple_of(block * 8, 8), 8)
        cells = [in_ref[f, at, :] for f in range(fields)]
        total = cells[0]
        for f in range(1, fields):
            total = total + cells[f]
        ensemble = total * (1.0 / fields)
        for f in range(fields):
            out_ref[f, at, :] = cells[f] - mixing * (cells[f] - ensemble)
        return carry

    lax.fori_loop(0, data // 8, one_block, 0)
    marks = jnp.zeros((8, LANES), F32)
    for f in range(fields):
        marks = marks + in_ref[f, data : data + 8, :] * float(2**f)
    code = [jnp.max(marks[z : z + 1, :]).astype(jnp.int32) for z in range(planes)]
    count = jnp.int32(0)
    for z in range(planes):
        for f in range(fields):
            list_ref[count] = f * planes + z
            count = count + ((code[z] >> f) & 1)
    tables = [ref[...] for ref in (pairs_ref, partner_ref, squares_ref, produced_ref)]

    @pl.loop(0, pl.cdiv(count, GROUP))
    def _(group):
        first = group * GROUP
        entries = [list_ref[jnp.minimum(first + j, count - 1)] for j in range(GROUP)]
        places = [(lax.div(e, planes), lax.rem(e, planes)) for e in entries]
        concent = jnp.concatenate([out_ref[f, pl.ds(z, species, stride=planes), :] for f, z in places], 1)
        concent = chemistry(concent, *tables)
        for j, (f, z) in enumerate(places):

            @pl.when(first + j < count)
            def _():
                out_ref[f, pl.ds(z, species, stride=planes), :] = concent[:, j * LANES : (j + 1) * LANES]


def home_kernel(in_ref, out_ref, rows_ref, sems):
    pieces, data, _ = in_ref.shape
    steps = sems.shape[0]
    part = data // steps
    copies = []
    for step in range(steps):
        size = part * pieces
        for y in range(pieces):
            at = pl.ds(step * size + y, part, stride=pieces)
            rows_ref[at, :] = in_ref[y, step * part : (step + 1) * part, :]
        at = pl.ds(step * size, size)
        copies.append(pltpu.make_async_copy(rows_ref.at[at], out_ref.at[at], sems.at[step]))
        copies[-1].start()
    for copy in copies:
        copy.wait()


def one_hot_rows(indices, count):
    return (indices[:, None] == jnp.arange(count, dtype=jnp.int32)[None, :]).astype(F32)


def reaction_tables(stoich, rates, species):
    highest = lax.Precision.HIGHEST
    rate = rates[:, None]
    one, two = one_hot_rows(stoich[0], species), one_hot_rows(stoich[1], species)
    produced = one_hot_rows(stoich[2], species) + one_hot_rows(stoich[3], species)
    both = one + two
    partner = jnp.dot((one * rate).T, two, precision=highest)
    squares = jnp.dot(produced.T, (0.5 * rate) * both, precision=highest)
    produced = (0.5 * produced).T.astype(BF16)
    return (
        weights(jnp.sqrt(rate) * both),
        weights(partner + partner.T),
        weights(squares),
        jnp.concatenate([produced, produced], 1),
    )


def per_device(scalars, diffusivity, velocity, mixing, rates, stoich, burn_tile, helper_slot):
    block = lax.axis_index("space")
    blocks = lax.axis_size("space")
    fields = lax.axis_size("field")
    cells = scalars[0]
    species, planes, rows, width = cells.shape
    data = species * planes
    field = lax.axis_index("field")
    core = field % 2

    def exchanged(ways):
        pairs = [
            (f * blocks + i, f * blocks + (i + ways[f % 2]) % blocks) for f in range(fields) for i in range(blocks)
        ]
        up = core if ways[1] == 1 else 1 - core
        plane = lax.dynamic_index_in_dim(cells, up * (planes - 1), 1, False)
        return lax.ppermute(plane, ("field", "space"), pairs).reshape(species * rows, width)

    first, second = exchanged((1, -1)), exchanged((-1, 1))
    tables = reaction_tables(stoich, rates, species)
    mixing_row = lax.dynamic_index_in_dim(mixing, field, 1, False)
    pieces = pl.pallas_call(
        local_kernel,
        out_shape=shape(rows, data + 8, width),
        in_specs=[SMEM] + [VMEM] * 3,
        out_specs=VMEM,
        scratch_shapes=[pltpu.VMEM((data * rows, width), F32)],
        compiler_params=LIMIT,
        name="local",
    )(burn_tile[0, block], cells, diffusivity, velocity)
    pieces = pl.pallas_call(
        halo_kernel,
        out_shape=shape(rows, data + 8, width),
        in_specs=[SMEM] + [VMEM] * 5,
        out_specs=VMEM,
        input_output_aliases={1: 0},
        compiler_params=LIMIT,
        name="halo",
    )(core.reshape(1), pieces, first, second, diffusivity, velocity)
    pieces, tables, mixing_row = lax.optimization_barrier((pieces, tables, mixing_row))
    pieces = lax.all_to_all(pieces, "field", 0, 0, tiled=True)
    pieces = pl.pallas_call(
        react_kernel,
        out_shape=shape(fields, data, width),
        in_specs=[VMEM] * 6,
        out_specs=VMEM,
        scratch_shapes=[pltpu.SMEM((fields * planes + 1,), jnp.int32)],
        compiler_params=LIMIT,
        name="react",
    )(pieces, mixing_row, *tables)
    pieces = lax.all_to_all(pieces, "field", 0, 0, tiled=True)
    updated = pl.pallas_call(
        home_kernel,
        out_shape=shape(data * rows, width),
        in_specs=[VMEM],
        out_specs=pl.BlockSpec(memory_space=pltpu.HBM),
        scratch_shapes=[pltpu.VMEM((data * rows, width), F32), pltpu.SemaphoreType.DMA((4,))],
        compiler_params=LIMIT,
        name="home",
    )(pieces)
    return updated.reshape(1, species, planes, rows, width)


def solution(mesh):
    return jax.shard_map(
        per_device,
        mesh=mesh,
        in_specs=(
            P("field", None, "space", None, None),
            P("space", None, None),
            P("space", None, None),
            P("space", None, None),
            P(),
            P(),
            P("field", None, None),
            P("field", None, None),
        ),
        out_specs=P("field", None, "space", None, None),
        check_vma=False,
    )
```

```python
import functools

import jax
import jax.numpy as jnp
from jax import lax
from jax.experimental import pallas as pl
from jax.experimental.pallas import tpu as pltpu
from jax.sharding import PartitionSpec as P

NSUB = 4
LANES = 128
GROUP = 12
F32 = jnp.float32
BF16 = jnp.bfloat16
VMEM = pl.BlockSpec(memory_space=pltpu.VMEM)
SMEM = pl.BlockSpec(memory_space=pltpu.SMEM)
LIMIT = pltpu.CompilerParams(vmem_limit_bytes=24 << 20)


def shape(*dims):
    return jax.ShapeDtypeStruct(dims, F32)


def local_kernel(
    block_ref, cells_ref, dif_ref, vel_ref, burn_ref, stoich_ref, rates_ref,
    out_ref, pairs_ref, partner_ref, squares_ref, produced_ref, rows_ref, flags_ref,
):
    species, planes, rows, _ = cells_ref.shape
    reaction_tables(stoich_ref, rates_ref, pairs_ref, partner_ref, squares_ref, produced_ref, species)
    tiles = planes * rows
    listed = burn_ref[pl.ds(block_ref[0], 1), :]
    match = lax.broadcasted_iota(jnp.int32, (tiles, listed.shape[1]), 0) == listed
    burning = jnp.max(jnp.where(match, 1.0, 0.0), axis=1, keepdims=True)
    flags_ref[...] = jnp.broadcast_to(burning, flags_ref.shape)
    last = planes - 1
    dif = [dif_ref[z] for z in range(planes)]
    vel = [vel_ref[z] for z in range(planes)]

    def one_species(s, carry):
        cells = [cells_ref[s, z] for z in range(planes)]
        for z in range(planes):
            center = cells[z]
            around = (
                pltpu.roll(center, 1, 1)
                + pltpu.roll(center, LANES - 1, 1)
                + pltpu.roll(center, 1, 0)
                + pltpu.roll(center, rows - 1, 0)
                - 6.0 * center
            )
            if z > 0:
                around = around + cells[z - 1]
            if z < last:
                around = around + cells[z + 1]
            drift = cells[z - 1] - center if z > 0 else -center
            start = pl.multiple_of((s * planes + z) * rows, rows)
            rows_ref[pl.ds(start, rows), :] = center + dif[z] * around + vel[z] * drift
        return carry

    lax.fori_loop(0, species, one_species, 0, unroll=4)
    data = species * planes
    for y in range(rows):
        out_ref[y, 0:data, :] = rows_ref[pl.ds(y, data, stride=rows), :]
        out_ref[y, data : data + 8, :] = jnp.zeros((8, LANES), F32)
        out_ref[y, data : data + planes, :] = flags_ref[pl.ds(y, planes, stride=rows), :]


def halo_kernel(up_ref, pieces_ref, first_ref, second_ref, dif_ref, vel_ref, out_ref):
    planes, rows, _ = dif_ref.shape
    species = first_ref.shape[0] // rows
    low = dif_ref[0] + vel_ref[0]
    high = dif_ref[planes - 1]

    def add(below_ref, above_ref):
        for y in range(rows):
            at = pl.ds(y, species, stride=rows)
            bottom, top = pl.ds(0, species, stride=planes), pl.ds(planes - 1, species, stride=planes)
            out_ref[y, bottom, :] = pieces_ref[y, bottom, :] + low[y : y + 1] * below_ref[at, :]
            out_ref[y, top, :] = pieces_ref[y, top, :] + high[y : y + 1] * above_ref[at, :]

    @pl.when(up_ref[0] == 0)
    def _():
        add(first_ref, second_ref)

    @pl.when(up_ref[0] == 1)
    def _():
        add(second_ref, first_ref)


def in_parts(x):
    high = x.astype(BF16)
    return high, (x - high.astype(F32)).astype(BF16)


def factors(x):
    high, low = in_parts(x)
    return jnp.concatenate([high, low, high], 0)


def weights(w):
    high, low = in_parts(w)
    return jnp.concatenate([high, high, low], 1)


def dot(a, b):
    return jnp.dot(a, b, preferred_element_type=F32)


def chemistry(concent, pairs, partner, squares, produced):
    substep = 1.0 / NSUB
    for repeat in range(NSUB):
        current = factors(concent)
        pair = dot(pairs, current)
        making = dot(produced, jnp.concatenate(in_parts(pair * pair), 0)) - dot(squares, factors(concent * concent))
        concent = (concent + substep * making) / (1.0 + substep * dot(partner, current))
    return concent


def react_kernel(in_ref, mix_ref, pairs_ref, partner_ref, squares_ref, produced_ref, out_ref, list_ref):
    fields, data, _ = out_ref.shape
    planes = mix_ref.shape[0]
    species = data // planes
    even = lax.broadcasted_iota(jnp.int32, (8, LANES), 0) % planes == 0
    mixing = jnp.where(even, mix_ref[0:1, :], mix_ref[1:2, :])

    def one_block(block, carry):
        at = pl.ds(pl.multiple_of(block * 8, 8), 8)
        cells = [in_ref[f, at, :] for f in range(fields)]
        total = cells[0]
        for f in range(1, fields):
            total = total + cells[f]
        ensemble = total * (1.0 / fields)
        for f in range(fields):
            out_ref[f, at, :] = cells[f] - mixing * (cells[f] - ensemble)
        return carry

    lax.fori_loop(0, data // 8, one_block, 0)
    marks = jnp.zeros((8, LANES), F32)
    for f in range(fields):
        marks = marks + in_ref[f, data : data + 8, :] * float(2**f)
    code = [jnp.max(marks[z : z + 1, :]).astype(jnp.int32) for z in range(planes)]
    count = jnp.int32(0)
    for z in range(planes):
        for f in range(fields):
            list_ref[count] = f * planes + z
            count = count + ((code[z] >> f) & 1)
    tables = [ref[...] for ref in (pairs_ref, partner_ref, squares_ref, produced_ref)]

    @pl.loop(0, pl.cdiv(count, GROUP))
    def _(group):
        first = group * GROUP
        entries = [list_ref[jnp.minimum(first + j, count - 1)] for j in range(GROUP)]
        places = [(lax.div(e, planes), lax.rem(e, planes)) for e in entries]
        concent = jnp.concatenate([out_ref[f, pl.ds(z, species, stride=planes), :] for f, z in places], 1)
        concent = chemistry(concent, *tables)
        for j, (f, z) in enumerate(places):

            @pl.when(first + j < count)
            def _():
                out_ref[f, pl.ds(z, species, stride=planes), :] = concent[:, j * LANES : (j + 1) * LANES]


def home_kernel(in_ref, out_ref, rows_ref, sems):
    pieces, data, _ = in_ref.shape
    steps = sems.shape[0]
    part = data // steps
    copies = []
    for step in range(steps):
        size = part * pieces
        for y in range(pieces):
            at = pl.ds(step * size + y, part, stride=pieces)
            rows_ref[at, :] = in_ref[y, step * part : (step + 1) * part, :]
        at = pl.ds(step * size, size)
        copies.append(pltpu.make_async_copy(rows_ref.at[at], out_ref.at[at], sems.at[step]))
        copies[-1].start()
    for copy in copies:
        copy.wait()


def reaction_tables(stoich_ref, rates_ref, pairs_ref, partner_ref, squares_ref, produced_ref, species):
    rates = rates_ref[...]
    each = lax.broadcasted_iota(jnp.int32, (species, rates.shape[1]), 0)
    one, two, three, four = [jnp.where(each == stoich_ref[i : i + 1, :], 1.0, 0.0) for i in range(4)]
    both, produced = one + two, three + four
    along = (((1,), (1,)), ((), ()))
    highest = lax.Precision.HIGHEST
    scaled = rates * both
    partner = lax.dot_general(rates * one, two, along, highest, F32) + lax.dot_general(rates * two, one, along, highest, F32)
    squares = lax.dot_general(produced, 0.5 * scaled, along, highest, F32)
    pairs = jnp.sqrt(rates) * both
    high = pairs.astype(BF16).astype(F32)
    pairs_ref[...] = jnp.concatenate([high, high, pairs - high], 0).T.astype(BF16)
    partner_ref[...] = weights(partner)
    squares_ref[...] = weights(squares)
    half = (0.5 * produced).astype(BF16)
    produced_ref[...] = jnp.concatenate([half, half], 1)


def per_device(scalars, diffusivity, velocity, mixing, rates, stoich, burn_tile, helper_slot):
    block = lax.axis_index("space")
    blocks = lax.axis_size("space")
    fields = lax.axis_size("field")
    cells = scalars[0]
    species, planes, rows, width = cells.shape
    data = species * planes
    field = lax.axis_index("field")
    core, parity = field % 2, block % 2
    up_first = (parity + core + 1) % 2

    def exchanged(near_core, up):
        pairs = []
        for f in range(fields):
            for i in range(blocks):
                step = 1 if (i % 2 == 0) == (f % 2 == near_core) else -1
                pairs.append((f * blocks + i, f * blocks + (i + step) % blocks))
        plane = lax.dynamic_index_in_dim(cells, up * (planes - 1), 1, False)
        return lax.ppermute(plane, ("field", "space"), pairs).reshape(species * rows, width)

    first, second = exchanged(0, up_first), exchanged(1, 1 - up_first)
    mixing_row = lax.dynamic_index_in_dim(mixing, field, 1, False)
    reactions = rates.shape[0]
    pieces, *tables = pl.pallas_call(
        local_kernel,
        out_shape=(
            shape(rows, data + 8, width),
            jax.ShapeDtypeStruct((reactions, 3 * species), BF16),
            jax.ShapeDtypeStruct((species, 3 * species), BF16),
            jax.ShapeDtypeStruct((species, 3 * species), BF16),
            jax.ShapeDtypeStruct((species, 2 * reactions), BF16),
        ),
        in_specs=[SMEM] + [VMEM] * 6,
        out_specs=[VMEM] * 5,
        scratch_shapes=[pltpu.VMEM((data * rows, width), F32), pltpu.VMEM((planes * rows, width), F32)],
        compiler_params=LIMIT,
        name="local",
    )(block.reshape(1), cells, diffusivity, velocity, burn_tile[0], stoich, rates[None])
    pieces = pl.pallas_call(
        halo_kernel,
        out_shape=shape(rows, data + 8, width),
        in_specs=[SMEM] + [VMEM] * 5,
        out_specs=VMEM,
        input_output_aliases={1: 0},
        compiler_params=LIMIT,
        name="halo",
    )(up_first.reshape(1), pieces, first, second, diffusivity, velocity)
    pieces, tables, mixing_row = lax.optimization_barrier((pieces, tables, mixing_row))
    pieces = lax.all_to_all(pieces, "field", 0, 0, tiled=True)
    pieces = pl.pallas_call(
        react_kernel,
        out_shape=shape(fields, data, width),
        in_specs=[VMEM] * 6,
        out_specs=VMEM,
        scratch_shapes=[pltpu.SMEM((fields * planes + 1,), jnp.int32)],
        compiler_params=LIMIT,
        name="react",
    )(pieces, mixing_row, *tables)
    pieces = lax.all_to_all(pieces, "field", 0, 0, tiled=True)
    updated = pl.pallas_call(
        home_kernel,
        out_shape=shape(data * rows, width),
        in_specs=[VMEM],
        out_specs=pl.BlockSpec(memory_space=pltpu.HBM),
        scratch_shapes=[pltpu.VMEM((data * rows, width), F32), pltpu.SemaphoreType.DMA((4,))],
        compiler_params=LIMIT,
        name="home",
    )(pieces)
    return updated.reshape(1, species, planes, rows, width)


def solution(mesh):
    return jax.shard_map(
        per_device,
        mesh=mesh,
        in_specs=(
            P("field", None, "space", None, None),
            P("space", None, None),
            P("space", None, None),
            P("space", None, None),
            P(),
            P(),
            P("field", None, None),
            P("field", None, None),
        ),
        out_specs=P("field", None, "space", None, None),
        check_vma=False,
    )
```

```python
import jax
import jax.numpy as jnp
from jax import lax
from jax.experimental import pallas as pl
from jax.experimental.pallas import tpu as pltpu
from jax.sharding import PartitionSpec as P


NSUB = 4
LANES = 128
GROUP = 12
DEPTH = 16
F32 = jnp.float32
BF16 = jnp.bfloat16
VMEM = pl.BlockSpec(memory_space=pltpu.VMEM)
SMEM = pl.BlockSpec(memory_space=pltpu.SMEM)
LIMIT = pltpu.CompilerParams(vmem_limit_bytes=24 << 20)


def shape(*dims):
    return jax.ShapeDtypeStruct(dims, F32)


def local_kernel(
    block_ref, cells_ref, dif_ref, vel_ref, burn_ref, stoich_ref, rates_ref,
    out_ref, pairs_ref, partner_ref, squares_ref, produced_ref, rows_ref, flags_ref,
):
    species, planes, rows, _ = cells_ref.shape
    reaction_tables(stoich_ref, rates_ref, pairs_ref, partner_ref, squares_ref, produced_ref, species)
    tiles = planes * rows
    listed = burn_ref[pl.ds(block_ref[0], 1), :]
    match = lax.broadcasted_iota(jnp.int32, (tiles, listed.shape[1]), 0) == listed
    burning = jnp.max(jnp.where(match, 1.0, 0.0), axis=1, keepdims=True)
    flags_ref[...] = jnp.broadcast_to(burning, flags_ref.shape)
    last = planes - 1
    dif = [dif_ref[z] for z in range(planes)]
    vel = [vel_ref[z] for z in range(planes)]

    def one_species(s, carry):
        cells = [cells_ref[s, z] for z in range(planes)]
        for z in range(planes):
            center = cells[z]
            around = (
                pltpu.roll(center, 1, 1)
                + pltpu.roll(center, LANES - 1, 1)
                + pltpu.roll(center, 1, 0)
                + pltpu.roll(center, rows - 1, 0)
                - 6.0 * center
            )
            if z > 0:
                around = around + cells[z - 1]
            if z < last:
                around = around + cells[z + 1]
            drift = cells[z - 1] - center if z > 0 else -center
            start = pl.multiple_of((s * planes + z) * rows, rows)
            rows_ref[pl.ds(start, rows), :] = center + dif[z] * around + vel[z] * drift
        return carry

    lax.fori_loop(0, species, one_species, 0, unroll=4)
    data = species * planes
    for y in range(rows):
        out_ref[y, 0:data, :] = rows_ref[pl.ds(y, data, stride=rows), :]
        out_ref[y, data : data + 8, :] = jnp.zeros((8, LANES), F32)
        out_ref[y, data : data + planes, :] = flags_ref[pl.ds(y, planes, stride=rows), :]


def halo_kernel(odd_ref, late_ref, pieces_ref, early_near_ref, across_ref, late_near_ref, dif_ref, vel_ref, out_ref):
    planes, rows, _ = dif_ref.shape
    species = across_ref.shape[0] // rows
    low = dif_ref[0] + vel_ref[0]
    high = dif_ref[planes - 1]

    def add(below_ref, above_ref):
        for y in range(rows):
            at = pl.ds(y, species, stride=rows)
            bottom, top = pl.ds(0, species, stride=planes), pl.ds(planes - 1, species, stride=planes)
            out_ref[y, bottom, :] = pieces_ref[y, bottom, :] + low[y : y + 1] * below_ref[at, :]
            out_ref[y, top, :] = pieces_ref[y, top, :] + high[y : y + 1] * above_ref[at, :]

    for late, near_ref in enumerate((early_near_ref, late_near_ref)):

        @pl.when((odd_ref[0] == 0) & (late_ref[0] == late))
        def _():
            add(across_ref, near_ref)

        @pl.when((odd_ref[0] == 1) & (late_ref[0] == late))
        def _():
            add(near_ref, across_ref)


def in_parts(x):
    high = x.astype(BF16)
    return high, (x - high.astype(F32)).astype(BF16)


def factors(x):
    high, low = in_parts(x)
    return jnp.concatenate([high, low, high], 0)


def weights(w):
    high, low = in_parts(w)
    return jnp.concatenate([high, high, low], 1)


def dot(a, b):
    return jnp.dot(a, b, preferred_element_type=F32)


def chemistry(concent, pairs, partner, squares, produced):
    substep = 1.0 / NSUB
    for _ in range(NSUB):
        current = factors(concent)
        pair = dot(pairs, current)
        making = dot(produced, jnp.concatenate(in_parts(pair * pair), 0)) - dot(squares, factors(concent * concent))
        concent = (concent + substep * making) / (1.0 + substep * dot(partner, current))
    return concent


def react_kernel(in_ref, mix_ref, pairs_ref, partner_ref, squares_ref, produced_ref, out_ref, list_ref):
    fields, data, _ = out_ref.shape
    planes = mix_ref.shape[0]
    species = data // planes
    even = lax.broadcasted_iota(jnp.int32, (8, LANES), 0) % planes == 0
    mixing = jnp.where(even, mix_ref[0:1, :], mix_ref[1:2, :])

    def one_block(block, carry):
        at = pl.ds(pl.multiple_of(block * 8, 8), 8)
        cells = [in_ref[f, at, :] for f in range(fields)]
        total = cells[0]
        for f in range(1, fields):
            total = total + cells[f]
        ensemble = total * (1.0 / fields)
        for f in range(fields):
            out_ref[f, at, :] = cells[f] - mixing * (cells[f] - ensemble)
        return carry

    lax.fori_loop(0, data // 8, one_block, 0)
    marks = jnp.zeros((8, LANES), F32)
    for f in range(fields):
        marks = marks + in_ref[f, data : data + 8, :] * float(2**f)
    code = [jnp.max(marks[z : z + 1, :]).astype(jnp.int32) for z in range(planes)]
    count = jnp.int32(0)
    for z in range(planes):
        for f in range(fields):
            list_ref[count] = f * planes + z
            count = count + ((code[z] >> f) & 1)
    tables = [ref[...] for ref in (pairs_ref, partner_ref, squares_ref, produced_ref)]

    @pl.loop(0, pl.cdiv(count, GROUP))
    def _(group):
        first = group * GROUP
        entries = [list_ref[jnp.minimum(first + j, count - 1)] for j in range(GROUP)]
        places = [(lax.div(e, planes), lax.rem(e, planes)) for e in entries]
        concent = jnp.concatenate([out_ref[f, pl.ds(z, species, stride=planes), :] for f, z in places], 1)
        concent = chemistry(concent, *tables)
        for j, (f, z) in enumerate(places):

            @pl.when(first + j < count)
            def _():
                out_ref[f, pl.ds(z, species, stride=planes), :] = concent[:, j * LANES : (j + 1) * LANES]


def home_kernel(in_ref, out_ref, rows_ref, sems):
    pieces, data, _ = in_ref.shape
    steps = sems.shape[0]
    part = data // steps
    copies = []
    for step in range(steps):
        size = part * pieces
        for y in range(pieces):
            at = pl.ds(step * size + y, part, stride=pieces)
            rows_ref[at, :] = in_ref[y, step * part : (step + 1) * part, :]
        at = pl.ds(step * size, size)
        copies.append(pltpu.make_async_copy(rows_ref.at[at], out_ref.at[at], sems.at[step]))
        copies[-1].start()
    for copy in copies:
        copy.wait()


def reaction_tables(stoich_ref, rates_ref, pairs_ref, partner_ref, squares_ref, produced_ref, species):
    rates = rates_ref[...]
    each = lax.broadcasted_iota(jnp.int32, (species, rates.shape[1]), 0)
    one, two, three, four = [jnp.where(each == stoich_ref[i : i + 1, :], 1.0, 0.0) for i in range(4)]
    both, produced = one + two, three + four
    along = (((1,), (1,)), ((), ()))
    highest = lax.Precision.HIGHEST
    scaled = rates * both
    partner = lax.dot_general(rates * one, two, along, highest, F32) + lax.dot_general(rates * two, one, along, highest, F32)
    squares = lax.dot_general(produced, 0.5 * scaled, along, highest, F32)
    pairs = jnp.sqrt(rates) * both
    high = pairs.astype(BF16).astype(F32)
    pairs_ref[...] = jnp.concatenate([high, high, pairs - high], 0).T.astype(BF16)
    partner_ref[...] = weights(partner)
    squares_ref[...] = weights(squares)
    half = (0.5 * produced).astype(BF16)
    produced_ref[...] = jnp.concatenate([half, half], 1)


def per_device(scalars, diffusivity, velocity, mixing, rates, stoich, burn_tile, helper_slot):
    block = lax.axis_index("space")
    blocks = lax.axis_size("space")
    fields = lax.axis_size("field")
    cells = scalars[0]
    species, planes, rows, width = cells.shape
    data = species * planes
    field = lax.axis_index("field")
    odd = block % 2
    late = (block % DEPTH) // (DEPTH // 2)
    near_plane = lax.dynamic_index_in_dim(cells, (1 - odd) * (planes - 1), 1, False)
    across_plane = lax.dynamic_index_in_dim(cells, odd * (planes - 1), 1, False)
    near_pairs = [(i, i ^ 1) for i in range(blocks)]
    half = [i % DEPTH < DEPTH // 2 for i in range(blocks)]
    across_pairs = [(i, (i + 1 if i % 2 else i - 1) % blocks) for i in range(blocks)]
    early_near = lax.ppermute(near_plane, "space", [p for p in near_pairs if half[p[0]]])
    across = lax.ppermute(across_plane, "space", across_pairs)
    late_near = lax.ppermute(near_plane, "space", [p for p in near_pairs if not half[p[0]]])
    received = [x.reshape(species * rows, width) for x in (early_near, across, late_near)]
    mixing_row = lax.dynamic_index_in_dim(mixing, field, 1, False)
    reactions = rates.shape[0]
    pieces, *tables = pl.pallas_call(
        local_kernel,
        out_shape=(
            shape(rows, data + 8, width),
            jax.ShapeDtypeStruct((reactions, 3 * species), BF16),
            jax.ShapeDtypeStruct((species, 3 * species), BF16),
            jax.ShapeDtypeStruct((species, 3 * species), BF16),
            jax.ShapeDtypeStruct((species, 2 * reactions), BF16),
        ),
        in_specs=[SMEM] + [VMEM] * 6,
        out_specs=[VMEM] * 5,
        scratch_shapes=[pltpu.VMEM((data * rows, width), F32), pltpu.VMEM((planes * rows, width), F32)],
        compiler_params=LIMIT,
        name="local",
    )(block.reshape(1), cells, diffusivity, velocity, burn_tile[0], stoich, rates[None])
    pieces = pl.pallas_call(
        halo_kernel,
        out_shape=shape(rows, data + 8, width),
        in_specs=[SMEM] * 2 + [VMEM] * 6,
        out_specs=VMEM,
        input_output_aliases={2: 0},
        compiler_params=LIMIT,
        name="halo",
    )(odd.reshape(1), late.reshape(1), pieces, *received, diffusivity, velocity)
    pieces, tables, mixing_row = lax.optimization_barrier((pieces, tables, mixing_row))
    pieces = lax.all_to_all(pieces, "field", 0, 0, tiled=True)
    pieces = pl.pallas_call(
        react_kernel,
        out_shape=shape(fields, data, width),
        in_specs=[VMEM] * 6,
        out_specs=VMEM,
        scratch_shapes=[pltpu.SMEM((fields * planes + 1,), jnp.int32)],
        compiler_params=LIMIT,
        name="react",
    )(pieces, mixing_row, *tables)
    pieces = lax.all_to_all(pieces, "field", 0, 0, tiled=True)
    updated = pl.pallas_call(
        home_kernel,
        out_shape=shape(data * rows, width),
        in_specs=[VMEM],
        out_specs=pl.BlockSpec(memory_space=pltpu.HBM),
        scratch_shapes=[pltpu.VMEM((data * rows, width), F32), pltpu.SemaphoreType.DMA((4,))],
        compiler_params=LIMIT,
        name="home",
    )(pieces)
    return updated.reshape(1, species, planes, rows, width)


def solution(mesh):
    return jax.shard_map(
        per_device,
        mesh=mesh,
        in_specs=(
            P("field", None, "space", None, None),
            P("space", None, None),
            P("space", None, None),
            P("space", None, None),
            P(),
            P(),
            P("field", None, None),
            P("field", None, None),
        ),
        out_specs=P("field", None, "space", None, None),
        check_vma=False,
    )
```

```python
import functools

import jax
import jax.numpy as jnp
from jax import lax
from jax.experimental import pallas as pl
from jax.experimental.pallas import tpu as pltpu
from jax.sharding import PartitionSpec as P


NSUB = 4
LANES = 128
GROUP = 12
DEPTH = 16
CORES = 2
F32 = jnp.float32
BF16 = jnp.bfloat16
VMEM = pl.BlockSpec(memory_space=pltpu.VMEM)
SMEM = pl.BlockSpec(memory_space=pltpu.SMEM)
LIMIT = pltpu.CompilerParams(vmem_limit_bytes=24 << 20)


def shape(*dims):
    return jax.ShapeDtypeStruct(dims, F32)


def local_kernel(
    block_ref, cells_ref, dif_ref, vel_ref, burn_ref, stoich_ref, rates_ref,
    out_ref, pairs_ref, partner_ref, squares_ref, produced_ref, rows_ref, flags_ref,
):
    species, planes, rows, _ = cells_ref.shape
    reaction_tables(stoich_ref, rates_ref, pairs_ref, partner_ref, squares_ref, produced_ref, species)
    tiles = planes * rows
    listed = burn_ref[pl.ds(block_ref[0], 1), :]
    match = lax.broadcasted_iota(jnp.int32, (tiles, listed.shape[1]), 0) == listed
    burning = jnp.max(jnp.where(match, 1.0, 0.0), axis=1, keepdims=True)
    flags_ref[...] = jnp.broadcast_to(burning, flags_ref.shape)
    last = planes - 1
    dif = [dif_ref[z] for z in range(planes)]
    vel = [vel_ref[z] for z in range(planes)]

    def one_species(s, carry):
        cells = [cells_ref[s, z] for z in range(planes)]
        for z in range(planes):
            center = cells[z]
            around = (
                pltpu.roll(center, 1, 1)
                + pltpu.roll(center, LANES - 1, 1)
                + pltpu.roll(center, 1, 0)
                + pltpu.roll(center, rows - 1, 0)
                - 6.0 * center
            )
            if z > 0:
                around = around + cells[z - 1]
            if z < last:
                around = around + cells[z + 1]
            drift = cells[z - 1] - center if z > 0 else -center
            start = pl.multiple_of((s * planes + z) * rows, rows)
            rows_ref[pl.ds(start, rows), :] = center + dif[z] * around + vel[z] * drift
        return carry

    lax.fori_loop(0, species, one_species, 0, unroll=4)
    data = species * planes
    pieces = out_ref.shape[0]
    share = rows // pieces
    for piece in range(pieces):
        out_ref[piece, share * data :, :] = jnp.zeros((8, LANES), F32)
        for r in range(share):
            y = piece * share + r
            out_ref[piece, r * data : (r + 1) * data, :] = rows_ref[pl.ds(y, data, stride=rows), :]
            flag = share * data + r * planes
            out_ref[piece, flag : flag + planes, :] = flags_ref[pl.ds(y, planes, stride=rows), :]


def halo_kernel(odd_ref, late_ref, pieces_ref, early_near_ref, across_ref, late_near_ref, dif_ref, vel_ref, out_ref):
    planes, rows, _ = dif_ref.shape
    species = across_ref.shape[0] // rows
    share = rows // out_ref.shape[0]
    low = dif_ref[0] + vel_ref[0]
    high = dif_ref[planes - 1]

    def add(below_ref, above_ref):
        for y in range(rows):
            at = pl.ds(y, species, stride=rows)
            piece, start = y // share, y % share * species * planes
            bottom, top = pl.ds(start, species, stride=planes), pl.ds(start + planes - 1, species, stride=planes)
            out_ref[piece, bottom, :] = pieces_ref[piece, bottom, :] + low[y : y + 1] * below_ref[at, :]
            out_ref[piece, top, :] = pieces_ref[piece, top, :] + high[y : y + 1] * above_ref[at, :]

    for late, near_ref in enumerate((early_near_ref, late_near_ref)):

        @pl.when((odd_ref[0] == 0) & (late_ref[0] == late))
        def _():
            add(across_ref, near_ref)

        @pl.when((odd_ref[0] == 1) & (late_ref[0] == late))
        def _():
            add(near_ref, across_ref)


def in_parts(x):
    high = x.astype(BF16)
    return high, (x - high.astype(F32)).astype(BF16)


def factors(x):
    high, low = in_parts(x)
    return jnp.concatenate([high, low, high], 0)


def weights(w):
    high, low = in_parts(w)
    return jnp.concatenate([high, high, low], 1)


def dot(a, b):
    return jnp.dot(a, b, preferred_element_type=F32)


def chemistry(concent, pairs, partner, squares, produced):
    substep = 1.0 / NSUB
    for _ in range(NSUB):
        current = factors(concent)
        pair = dot(pairs, current)
        making = dot(produced, jnp.concatenate(in_parts(pair * pair), 0)) - dot(squares, factors(concent * concent))
        concent = (concent + substep * making) / (1.0 + substep * dot(partner, current))
    return concent


def sum_kernel(in_ref, out_ref):
    @pl.loop(0, out_ref.shape[0] // 8)
    def _(block):
        at = pl.ds(pl.multiple_of(block * 8, 8), 8)
        total = in_ref[0, at, :]
        for f in range(1, in_ref.shape[0]):
            total = total + in_ref[f, at, :]
        out_ref[at, :] = total


def react_kernel(
    in_ref, own_ref, other_ref, mix_ref, pairs_ref, partner_ref, squares_ref, produced_ref, out_ref, list_ref
):
    fields, size, _ = out_ref.shape
    planes, share, _ = mix_ref.shape
    data = size // share
    species = data // planes
    even = lax.broadcasted_iota(jnp.int32, (8, LANES), 0) % planes == 0
    for r in range(share):
        mixing = jnp.where(even, mix_ref[0, r : r + 1, :], mix_ref[1, r : r + 1, :])

        def one_block(block, carry):
            at = pl.ds(pl.multiple_of(r * data + block * 8, 8), 8)
            ensemble = (own_ref[at, :] + other_ref[at, :]) * (0.5 / fields)
            for f in range(fields):
                cells = in_ref[f, at, :]
                out_ref[f, at, :] = cells - mixing * (cells - ensemble)
            return carry

        lax.fori_loop(0, data // 8, one_block, 0)
    marks = jnp.zeros((8, LANES), F32)
    for f in range(fields):
        marks = marks + in_ref[f, size : size + 8, :] * float(2**f)
    count = jnp.int32(0)
    for start in range(share * planes):
        code = jnp.max(marks[start : start + 1, :]).astype(jnp.int32)
        for f in range(fields):
            list_ref[count] = f * share * planes + start
            count = count + ((code >> f) & 1)
    tables = [ref[...] for ref in (pairs_ref, partner_ref, squares_ref, produced_ref)]

    @pl.loop(0, pl.cdiv(count, GROUP))
    def _(group):
        first = group * GROUP
        places = []
        for j in range(GROUP):
            entry = list_ref[jnp.minimum(first + j, count - 1)]
            f, rest = lax.div(entry, share * planes), lax.rem(entry, share * planes)
            places.append((f, lax.div(rest, planes) * data + lax.rem(rest, planes)))
        concent = jnp.concatenate([out_ref[f, pl.ds(start, species, stride=planes), :] for f, start in places], 1)
        concent = chemistry(concent, *tables)
        for j, (f, start) in enumerate(places):

            @pl.when(first + j < count)
            def _():
                out_ref[f, pl.ds(start, species, stride=planes), :] = concent[:, j * LANES : (j + 1) * LANES]


def home_kernel(rows, in_ref, out_ref, rows_ref, sems):
    pieces, size, _ = in_ref.shape
    share = rows // pieces
    data = size // share
    steps = sems.shape[0]
    part = data // steps
    copies = []
    for step in range(steps):
        for y in range(rows):
            start = y % share * data + step * part
            rows_ref[pl.ds(step * part * rows + y, part, stride=rows), :] = in_ref[y // share, start : start + part, :]
        at = pl.ds(step * part * rows, part * rows)
        copies.append(pltpu.make_async_copy(rows_ref.at[at], out_ref.at[at], sems.at[step]))
        copies[-1].start()
    for copy in copies:
        copy.wait()


def reaction_tables(stoich_ref, rates_ref, pairs_ref, partner_ref, squares_ref, produced_ref, species):
    rates = rates_ref[...]
    each = lax.broadcasted_iota(jnp.int32, (species, rates.shape[1]), 0)
    one, two, three, four = [jnp.where(each == stoich_ref[i : i + 1, :], 1.0, 0.0) for i in range(4)]
    both, produced = one + two, three + four
    along = (((1,), (1,)), ((), ()))
    highest = lax.Precision.HIGHEST
    scaled = rates * both
    partner = lax.dot_general(rates * one, two, along, highest, F32) + lax.dot_general(rates * two, one, along, highest, F32)
    squares = lax.dot_general(produced, 0.5 * scaled, along, highest, F32)
    pairs = jnp.sqrt(rates) * both
    high = pairs.astype(BF16).astype(F32)
    pairs_ref[...] = jnp.concatenate([high, high, pairs - high], 0).T.astype(BF16)
    partner_ref[...] = weights(partner)
    squares_ref[...] = weights(squares)
    half = (0.5 * produced).astype(BF16)
    produced_ref[...] = jnp.concatenate([half, half], 1)


def per_device(scalars, diffusivity, velocity, mixing, rates, stoich, burn_tile, helper_slot):
    block = lax.axis_index("space")
    blocks = lax.axis_size("space")
    fields = lax.axis_size("field")
    cells = scalars[0]
    species, planes, rows, width = cells.shape
    data = species * planes
    field = lax.axis_index("field")
    odd = block % 2
    late = (block % DEPTH) // (DEPTH // 2)
    near_plane = lax.dynamic_index_in_dim(cells, (1 - odd) * (planes - 1), 1, False)
    across_plane = lax.dynamic_index_in_dim(cells, odd * (planes - 1), 1, False)
    near_pairs = [(i, i ^ 1) for i in range(blocks)]
    half = [i % DEPTH < DEPTH // 2 for i in range(blocks)]
    across_pairs = [(i, (i + 1 if i % 2 else i - 1) % blocks) for i in range(blocks)]
    early_near = lax.ppermute(near_plane, "space", [p for p in near_pairs if half[p[0]]])
    across = lax.ppermute(across_plane, "space", across_pairs)
    late_near = lax.ppermute(near_plane, "space", [p for p in near_pairs if not half[p[0]]])
    received = [x.reshape(species * rows, width) for x in (early_near, across, late_near)]
    chips = fields // CORES
    share = rows // chips
    groups = [[chip * CORES + core for chip in range(chips)] for core in range(CORES)]
    partners = [(i, i ^ 1) for i in range(fields)]
    mixing_rows = lax.dynamic_slice_in_dim(mixing, field // CORES * share, share, 1)
    reactions = rates.shape[0]
    pieces, *tables = pl.pallas_call(
        local_kernel,
        out_shape=(
            shape(chips, share * data + 8, width),
            jax.ShapeDtypeStruct((reactions, 3 * species), BF16),
            jax.ShapeDtypeStruct((species, 3 * species), BF16),
            jax.ShapeDtypeStruct((species, 3 * species), BF16),
            jax.ShapeDtypeStruct((species, 2 * reactions), BF16),
        ),
        in_specs=[SMEM] + [VMEM] * 6,
        out_specs=[VMEM] * 5,
        scratch_shapes=[pltpu.VMEM((data * rows, width), F32), pltpu.VMEM((planes * rows, width), F32)],
        compiler_params=LIMIT,
        name="local",
    )(block.reshape(1), cells, diffusivity, velocity, burn_tile[0], stoich, rates[None])
    pieces = pl.pallas_call(
        halo_kernel,
        out_shape=shape(chips, share * data + 8, width),
        in_specs=[SMEM] * 2 + [VMEM] * 6,
        out_specs=VMEM,
        input_output_aliases={2: 0},
        compiler_params=LIMIT,
        name="halo",
    )(odd.reshape(1), late.reshape(1), pieces, *received, diffusivity, velocity)
    pieces, tables, mixing_rows = lax.optimization_barrier((pieces, tables, mixing_rows))
    pieces = lax.all_to_all(pieces, "field", 0, 0, axis_index_groups=groups, tiled=True)
    own = pl.pallas_call(
        sum_kernel,
        out_shape=shape(share * data, width),
        in_specs=[VMEM],
        out_specs=VMEM,
        compiler_params=LIMIT,
        name="sum",
    )(pieces)
    other = lax.ppermute(own, "field", partners)
    pieces = pl.pallas_call(
        react_kernel,
        out_shape=shape(chips, share * data, width),
        in_specs=[VMEM] * 8,
        out_specs=VMEM,
        scratch_shapes=[pltpu.SMEM((chips * share * planes + 1,), jnp.int32)],
        compiler_params=LIMIT,
        name="react",
    )(pieces, own, other, mixing_rows, *tables)
    pieces = lax.all_to_all(pieces, "field", 0, 0, axis_index_groups=groups, tiled=True)
    updated = pl.pallas_call(
        functools.partial(home_kernel, rows),
        out_shape=shape(data * rows, width),
        in_specs=[VMEM],
        out_specs=pl.BlockSpec(memory_space=pltpu.HBM),
        scratch_shapes=[pltpu.VMEM((data * rows, width), F32), pltpu.SemaphoreType.DMA((4,))],
        compiler_params=LIMIT,
        name="home",
    )(pieces)
    return updated.reshape(1, species, planes, rows, width)


def solution(mesh):
    return jax.shard_map(
        per_device,
        mesh=mesh,
        in_specs=(
            P("field", None, "space", None, None),
            P("space", None, None),
            P("space", None, None),
            P("space", None, None),
            P(),
            P(),
            P("field", None, None),
            P("field", None, None),
        ),
        out_specs=P("field", None, "space", None, None),
        check_vma=False,
    )
```

```python
import jax
import jax.numpy as jnp
from jax import lax
from jax.experimental import pallas as pl
from jax.experimental.pallas import tpu as pltpu
from jax.sharding import PartitionSpec as P


NSUB = 4
LANES = 128
GROUPS = 10, 12
DEPTH = 16
F32 = jnp.float32
BF16 = jnp.bfloat16
VMEM = pl.BlockSpec(memory_space=pltpu.VMEM)
SMEM = pl.BlockSpec(memory_space=pltpu.SMEM)
LIMIT = pltpu.CompilerParams(vmem_limit_bytes=24 << 20)


def shape(*dims):
    return jax.ShapeDtypeStruct(dims, F32)


def local_kernel(
    block_ref, cells_ref, dif_ref, vel_ref, burn_ref, stoich_ref, rates_ref,
    out_ref, pairs_ref, partner_ref, squares_ref, produced_ref, rows_ref, flags_ref,
):
    species, planes, rows, _ = cells_ref.shape
    reaction_tables(stoich_ref, rates_ref, pairs_ref, partner_ref, squares_ref, produced_ref, species)
    tiles = planes * rows
    listed = burn_ref[pl.ds(block_ref[0], 1), :]
    match = lax.broadcasted_iota(jnp.int32, (tiles, listed.shape[1]), 0) == listed
    burning = jnp.max(jnp.where(match, 1.0, 0.0), axis=1, keepdims=True)
    flags_ref[...] = jnp.broadcast_to(burning, flags_ref.shape)
    last = planes - 1
    dif = [dif_ref[z] for z in range(planes)]
    vel = [vel_ref[z] for z in range(planes)]

    def one_species(s, carry):
        cells = [cells_ref[s, z] for z in range(planes)]
        for z in range(planes):
            center = cells[z]
            around = (
                pltpu.roll(center, 1, 1)
                + pltpu.roll(center, LANES - 1, 1)
                + pltpu.roll(center, 1, 0)
                + pltpu.roll(center, rows - 1, 0)
                - 6.0 * center
            )
            if z > 0:
                around = around + cells[z - 1]
            if z < last:
                around = around + cells[z + 1]
            drift = cells[z - 1] - center if z > 0 else -center
            start = pl.multiple_of((s * planes + z) * rows, rows)
            rows_ref[pl.ds(start, rows), :] = center + dif[z] * around + vel[z] * drift
        return carry

    lax.fori_loop(0, species, one_species, 0, unroll=4)
    data = species * planes
    for y in range(rows):
        out_ref[y, 0:data, :] = rows_ref[pl.ds(y, data, stride=rows), :]
        out_ref[y, data : data + 8, :] = jnp.zeros((8, LANES), F32)
        out_ref[y, data : data + planes, :] = flags_ref[pl.ds(y, planes, stride=rows), :]


def halo_kernel(odd_ref, late_ref, pieces_ref, early_near_ref, across_ref, late_near_ref, dif_ref, vel_ref, out_ref):
    planes, rows, _ = dif_ref.shape
    species = across_ref.shape[0] // rows
    low = dif_ref[0] + vel_ref[0]
    high = dif_ref[planes - 1]

    def add(below_ref, above_ref):
        for y in range(rows):
            at = pl.ds(y, species, stride=rows)
            bottom, top = pl.ds(0, species, stride=planes), pl.ds(planes - 1, species, stride=planes)
            out_ref[y, bottom, :] = pieces_ref[y, bottom, :] + low[y : y + 1] * below_ref[at, :]
            out_ref[y, top, :] = pieces_ref[y, top, :] + high[y : y + 1] * above_ref[at, :]
            out_ref[y, species * planes :, :] = pieces_ref[y, species * planes :, :]

    for late, near_ref in enumerate((early_near_ref, late_near_ref)):

        @pl.when((odd_ref[0] == 0) & (late_ref[0] == late))
        def _():
            add(across_ref, near_ref)

        @pl.when((odd_ref[0] == 1) & (late_ref[0] == late))
        def _():
            add(near_ref, across_ref)


def in_parts(x):
    high = x.astype(BF16)
    return high, (x - high.astype(F32)).astype(BF16)


def factors(x):
    high, low = in_parts(x)
    return jnp.concatenate([high, low, high], 0)


def weights(w):
    high, low = in_parts(w)
    return jnp.concatenate([high, high, low], 1)


def dot(a, b):
    return jnp.dot(a, b, preferred_element_type=F32)


def chemistry(concent, pairs, partner, squares, produced):
    substep = 1.0 / NSUB
    for _ in range(NSUB):
        current = factors(concent)
        pair = dot(pairs, current)
        making = dot(produced, jnp.concatenate(in_parts(pair * pair), 0)) - dot(squares, factors(concent * concent))
        concent = (concent + substep * making) / (1.0 + substep * dot(partner, current))
    return concent


def react_kernel(in_ref, mix_ref, pairs_ref, partner_ref, squares_ref, produced_ref, out_ref, list_ref):
    fields, data, _ = out_ref.shape
    planes = mix_ref.shape[0]
    species = data // planes
    even = lax.broadcasted_iota(jnp.int32, (8, LANES), 0) % planes == 0
    mixing = jnp.where(even, mix_ref[0:1, :], mix_ref[1:2, :])

    def one_block(block, carry):
        at = pl.ds(pl.multiple_of(block * 8, 8), 8)
        cells = [in_ref[f, at, :] for f in range(fields)]
        total = cells[0]
        for f in range(1, fields):
            total = total + cells[f]
        ensemble = total * (1.0 / fields)
        for f in range(fields):
            out_ref[f, at, :] = cells[f] - mixing * (cells[f] - ensemble)
        return carry

    lax.fori_loop(0, data // 8, one_block, 0)
    marks = jnp.zeros((8, LANES), F32)
    for f in range(fields):
        marks = marks + in_ref[f, data : data + 8, :] * float(2**f)
    code = [jnp.max(marks[z : z + 1, :]).astype(jnp.int32) for z in range(planes)]
    count = jnp.int32(0)
    for z in range(planes):
        for f in range(fields):
            list_ref[count] = f * planes + z
            count = count + ((code[z] >> f) & 1)
    tables = [ref[...] for ref in (pairs_ref, partner_ref, squares_ref, produced_ref)]

    def react(size):
        @pl.loop(0, pl.cdiv(count, size))
        def _(group):
            first = group * size
            entries = [list_ref[jnp.minimum(first + j, count - 1)] for j in range(size)]
            places = [(lax.div(e, planes), lax.rem(e, planes)) for e in entries]
            concent = jnp.concatenate([out_ref[f, pl.ds(z, species, stride=planes), :] for f, z in places], 1)
            concent = chemistry(concent, *tables)
            for j, (f, z) in enumerate(places):

                @pl.when(first + j < count)
                def _():
                    out_ref[f, pl.ds(z, species, stride=planes), :] = concent[:, j * LANES : (j + 1) * LANES]

    small, large = GROUPS

    @pl.when(count <= small)
    def _():
        react(small)

    @pl.when(count > small)
    def _():
        react(large)


def home_kernel(in_ref, out_ref, rows_ref, sems):
    pieces, data, _ = in_ref.shape
    steps = sems.shape[0]
    part = data // steps
    copies = []
    for step in range(steps):
        size = part * pieces
        for y in range(pieces):
            at = pl.ds(step * size + y, part, stride=pieces)
            rows_ref[at, :] = in_ref[y, step * part : (step + 1) * part, :]
        at = pl.ds(step * size, size)
        copies.append(pltpu.make_async_copy(rows_ref.at[at], out_ref.at[at], sems.at[step]))
        copies[-1].start()
    for copy in copies:
        copy.wait()


def reaction_tables(stoich_ref, rates_ref, pairs_ref, partner_ref, squares_ref, produced_ref, species):
    rates = rates_ref[...]
    each = lax.broadcasted_iota(jnp.int32, (species, rates.shape[1]), 0)
    one, two, three, four = [jnp.where(each == stoich_ref[i : i + 1, :], 1.0, 0.0) for i in range(4)]
    both, produced = one + two, three + four
    along = (((1,), (1,)), ((), ()))
    highest = lax.Precision.HIGHEST
    scaled = rates * both
    partner = lax.dot_general(rates * one, two, along, highest, F32) + lax.dot_general(rates * two, one, along, highest, F32)
    squares = lax.dot_general(produced, 0.5 * scaled, along, highest, F32)
    pairs = jnp.sqrt(rates) * both
    high = pairs.astype(BF16).astype(F32)
    pairs_ref[...] = jnp.concatenate([high, high, pairs - high], 0).T.astype(BF16)
    partner_ref[...] = weights(partner)
    squares_ref[...] = weights(squares)
    half = (0.5 * produced).astype(BF16)
    produced_ref[...] = jnp.concatenate([half, half], 1)


def per_device(scalars, diffusivity, velocity, mixing, rates, stoich, burn_tile, helper_slot):
    block = lax.axis_index("space")
    blocks = lax.axis_size("space")
    fields = lax.axis_size("field")
    cells = scalars[0]
    species, planes, rows, width = cells.shape
    data = species * planes
    field = lax.axis_index("field")
    odd = block % 2
    late = (block % DEPTH) // (DEPTH // 2)
    near_plane = lax.dynamic_index_in_dim(cells, (1 - odd) * (planes - 1), 1, False)
    across_plane = lax.dynamic_index_in_dim(cells, odd * (planes - 1), 1, False)
    near_pairs = [(i, i ^ 1) for i in range(blocks)]
    half = [i % DEPTH < DEPTH // 2 for i in range(blocks)]
    across_pairs = [(i, (i + 1 if i % 2 else i - 1) % blocks) for i in range(blocks)]
    early_near = lax.ppermute(near_plane, "space", [p for p in near_pairs if half[p[0]]])
    across = lax.ppermute(across_plane, "space", across_pairs)
    late_near = lax.ppermute(near_plane, "space", [p for p in near_pairs if not half[p[0]]])
    received = [x.reshape(species * rows, width) for x in (early_near, across, late_near)]
    mixing_row = lax.dynamic_index_in_dim(mixing, field, 1, False)
    reactions = rates.shape[0]
    pieces, *tables = pl.pallas_call(
        local_kernel,
        out_shape=(
            shape(rows, data + 8, width),
            jax.ShapeDtypeStruct((reactions, 3 * species), BF16),
            jax.ShapeDtypeStruct((species, 3 * species), BF16),
            jax.ShapeDtypeStruct((species, 3 * species), BF16),
            jax.ShapeDtypeStruct((species, 2 * reactions), BF16),
        ),
        in_specs=[SMEM] + [VMEM] * 6,
        out_specs=[VMEM] * 5,
        scratch_shapes=[pltpu.VMEM((data * rows, width), F32), pltpu.VMEM((planes * rows, width), F32)],
        compiler_params=LIMIT,
        name="local",
    )(block.reshape(1), cells, diffusivity, velocity, burn_tile[0], stoich, rates[None])
    pieces = pl.pallas_call(
        halo_kernel,
        out_shape=shape(rows, data + 8, width),
        in_specs=[SMEM] * 2 + [VMEM] * 6,
        out_specs=VMEM,
        input_output_aliases={2: 0},
        compiler_params=LIMIT,
        name="halo",
    )(odd.reshape(1), late.reshape(1), pieces, *received, diffusivity, velocity)
    pieces, tables, mixing_row = lax.optimization_barrier((pieces, tables, mixing_row))
    pieces = lax.all_to_all(pieces, "field", 0, 0, tiled=True)
    pieces = pl.pallas_call(
        react_kernel,
        out_shape=shape(fields, data, width),
        in_specs=[VMEM] * 6,
        out_specs=VMEM,
        scratch_shapes=[pltpu.SMEM((fields * planes + 1,), jnp.int32)],
        compiler_params=LIMIT,
        name="react",
    )(pieces, mixing_row, *tables)
    pieces = lax.all_to_all(pieces, "field", 0, 0, tiled=True)
    updated = pl.pallas_call(
        home_kernel,
        out_shape=shape(data * rows, width),
        in_specs=[VMEM],
        out_specs=pl.BlockSpec(memory_space=pltpu.HBM),
        scratch_shapes=[pltpu.VMEM((data * rows, width), F32), pltpu.SemaphoreType.DMA((4,))],
        compiler_params=LIMIT,
        name="home",
    )(pieces)
    return updated.reshape(1, species, planes, rows, width)


def solution(mesh):
    return jax.shard_map(
        per_device,
        mesh=mesh,
        in_specs=(
            P("field", None, "space", None, None),
            P("space", None, None),
            P("space", None, None),
            P("space", None, None),
            P(),
            P(),
            P("field", None, None),
            P("field", None, None),
        ),
        out_specs=P("field", None, "space", None, None),
        check_vma=False,
    )
```

```python
import jax
import jax.numpy as jnp
from jax import lax
from jax.experimental import pallas as pl
from jax.experimental.pallas import tpu as pltpu
from jax.sharding import PartitionSpec as P


NSUB = 4
LANES = 128
GROUPS = 10, 12
DEPTH = 16
F32 = jnp.float32
BF16 = jnp.bfloat16
VMEM = pl.BlockSpec(memory_space=pltpu.VMEM)
SMEM = pl.BlockSpec(memory_space=pltpu.SMEM)
LIMIT = pltpu.CompilerParams(vmem_limit_bytes=24 << 20)


def shape(*dims):
    return jax.ShapeDtypeStruct(dims, F32)


def local_kernel(
    block_ref, cells_ref, dif_ref, vel_ref, burn_ref, stoich_ref, rates_ref,
    out_ref, pairs_ref, partner_ref, squares_ref, produced_ref, rows_ref, flags_ref,
):
    species, planes, rows, _ = cells_ref.shape
    reaction_tables(stoich_ref, rates_ref, pairs_ref, partner_ref, squares_ref, produced_ref, species)
    tiles = planes * rows
    listed = burn_ref[pl.ds(block_ref[0], 1), :]
    match = lax.broadcasted_iota(jnp.int32, (tiles, listed.shape[1]), 0) == listed
    burning = jnp.max(jnp.where(match, 1.0, 0.0), axis=1, keepdims=True)
    flags_ref[...] = jnp.broadcast_to(burning, flags_ref.shape)
    last = planes - 1
    dif = [dif_ref[z] for z in range(planes)]
    vel = [vel_ref[z] for z in range(planes)]

    def one_species(s, carry):
        cells = [cells_ref[s, z] for z in range(planes)]
        for z in range(planes):
            center = cells[z]
            around = (
                pltpu.roll(center, 1, 1)
                + pltpu.roll(center, LANES - 1, 1)
                + pltpu.roll(center, 1, 0)
                + pltpu.roll(center, rows - 1, 0)
                - 6.0 * center
            )
            if z > 0:
                around = around + cells[z - 1]
            if z < last:
                around = around + cells[z + 1]
            drift = cells[z - 1] - center if z > 0 else -center
            start = pl.multiple_of((s * planes + z) * rows, rows)
            rows_ref[pl.ds(start, rows), :] = center + dif[z] * around + vel[z] * drift
        return carry

    lax.fori_loop(0, species, one_species, 0, unroll=4)
    data = species * planes
    for y in range(rows):
        out_ref[y, 0:data, :] = rows_ref[pl.ds(y, data, stride=rows), :]
        out_ref[y, data : data + 8, :] = jnp.zeros((8, LANES), F32)
        out_ref[y, data : data + planes, :] = flags_ref[pl.ds(y, planes, stride=rows), :]


def halo_kernel(odd_ref, late_ref, pieces_ref, early_near_ref, across_ref, late_near_ref, dif_ref, vel_ref, out_ref):
    planes, rows, _ = dif_ref.shape
    species = across_ref.shape[0] // rows
    low = dif_ref[0] + vel_ref[0]
    high = dif_ref[planes - 1]

    def add(below_ref, above_ref):
        for y in range(rows):
            at = pl.ds(y, species, stride=rows)
            bottom, top = pl.ds(0, species, stride=planes), pl.ds(planes - 1, species, stride=planes)
            out_ref[y, bottom, :] = pieces_ref[y, bottom, :] + low[y : y + 1] * below_ref[at, :]
            out_ref[y, top, :] = pieces_ref[y, top, :] + high[y : y + 1] * above_ref[at, :]
            out_ref[y, species * planes :, :] = pieces_ref[y, species * planes :, :]

    for late, near_ref in enumerate((early_near_ref, late_near_ref)):

        @pl.when((odd_ref[0] == 0) & (late_ref[0] == late))
        def _():
            add(across_ref, near_ref)

        @pl.when((odd_ref[0] == 1) & (late_ref[0] == late))
        def _():
            add(near_ref, across_ref)


def in_parts(x):
    high = x.astype(BF16)
    return high, (x - high.astype(F32)).astype(BF16)


def factors(x):
    high, low = in_parts(x)
    return jnp.concatenate([high, low, high], 0)


def weights(w):
    high, low = in_parts(w)
    return jnp.concatenate([high, high, low], 1)


def dot(a, b):
    return jnp.dot(a, b, preferred_element_type=F32)


def chemistry(concent, pairs, partner, squares, produced):
    substep = 1.0 / NSUB
    for _ in range(NSUB):
        current = factors(concent)
        pair = dot(pairs, current)
        making = dot(produced, jnp.concatenate(in_parts(pair * pair), 0)) - dot(squares, factors(concent * concent))
        concent = (concent + substep * making) / (1.0 + substep * dot(partner, current))
    return concent


def react_kernel(in_ref, mix_ref, pairs_ref, partner_ref, squares_ref, produced_ref, out_ref, list_ref):
    fields, data, _ = out_ref.shape
    planes = mix_ref.shape[0]
    species = data // planes
    even = lax.broadcasted_iota(jnp.int32, (8, LANES), 0) % planes == 0
    mixing = jnp.where(even, mix_ref[0:1, :], mix_ref[1:2, :])

    def one_block(block, carry):
        at = pl.ds(pl.multiple_of(block * 8, 8), 8)
        cells = [in_ref[f, at, :] for f in range(fields)]
        total = cells[0]
        for f in range(1, fields):
            total = total + cells[f]
        ensemble = total * (1.0 / fields)
        for f in range(fields):
            out_ref[f, at, :] = cells[f] - mixing * (cells[f] - ensemble)
        return carry

    lax.fori_loop(0, data // 8, one_block, 0)
    marks = jnp.zeros((8, LANES), F32)
    for f in range(fields):
        marks = marks + in_ref[f, data : data + 8, :] * float(2**f)
    code = [jnp.max(marks[z : z + 1, :]).astype(jnp.int32) for z in range(planes)]
    count = jnp.int32(0)
    for z in range(planes):
        for f in range(fields):
            list_ref[count] = f * planes + z
            count = count + ((code[z] >> f) & 1)
    tables = [ref[...] for ref in (pairs_ref, partner_ref, squares_ref, produced_ref)]

    def react(size):
        @pl.loop(0, pl.cdiv(count, size))
        def _(group):
            first = group * size
            entries = [list_ref[jnp.minimum(first + j, count - 1)] for j in range(size)]
            places = [(lax.div(e, planes), lax.rem(e, planes)) for e in entries]
            concent = jnp.concatenate([out_ref[f, pl.ds(z, species, stride=planes), :] for f, z in places], 1)
            concent = chemistry(concent, *tables)
            for j, (f, z) in enumerate(places):

                @pl.when(first + j < count)
                def _():
                    out_ref[f, pl.ds(z, species, stride=planes), :] = concent[:, j * LANES : (j + 1) * LANES]

    small, large = GROUPS

    @pl.when(count <= small)
    def _():
        react(small)

    @pl.when(count > small)
    def _():
        react(large)


def home_kernel(in_ref, out_ref, rows_ref, sems):
    pieces, data, _ = in_ref.shape
    steps = sems.shape[0]
    part = data // steps
    copies = []
    for step in range(steps):
        size = part * pieces
        for y in range(pieces):
            at = pl.ds(step * size + y, part, stride=pieces)
            rows_ref[at, :] = in_ref[y, step * part : (step + 1) * part, :]
        at = pl.ds(step * size, size)
        copies.append(pltpu.make_async_copy(rows_ref.at[at], out_ref.at[at], sems.at[step]))
        copies[-1].start()
    for copy in copies:
        copy.wait()


def reaction_tables(stoich_ref, rates_ref, pairs_ref, partner_ref, squares_ref, produced_ref, species):
    rates = rates_ref[...]
    each = lax.broadcasted_iota(jnp.int32, (species, rates.shape[1]), 0)
    one, two, three, four = [jnp.where(each == stoich_ref[i : i + 1, :], 1.0, 0.0) for i in range(4)]
    both, produced = one + two, three + four
    along = (((1,), (1,)), ((), ()))
    highest = lax.Precision.HIGHEST
    scaled = rates * both
    partner = lax.dot_general(rates * one, two, along, highest, F32) + lax.dot_general(rates * two, one, along, highest, F32)
    squares = lax.dot_general(produced, 0.5 * scaled, along, highest, F32)
    pairs = jnp.sqrt(rates) * both
    high = pairs.astype(BF16).astype(F32)
    pairs_ref[...] = jnp.concatenate([high, high, pairs - high], 0).T.astype(BF16)
    partner_ref[...] = weights(partner)
    squares_ref[...] = weights(squares)
    half = (0.5 * produced).astype(BF16)
    produced_ref[...] = jnp.concatenate([half, half], 1)


def per_device(scalars, diffusivity, velocity, mixing, rates, stoich, burn_tile, helper_slot):
    block = lax.axis_index("space")
    blocks = lax.axis_size("space")
    fields = lax.axis_size("field")
    cells = scalars[0]
    species, planes, rows, width = cells.shape
    data = species * planes
    field = lax.axis_index("field")
    odd = block % 2
    place = block % DEPTH
    late = ((place >= DEPTH // 2) & (place < DEPTH - 1)).astype(jnp.int32)
    near_plane = lax.dynamic_index_in_dim(cells, (1 - odd) * (planes - 1), 1, False)
    across_plane = lax.dynamic_index_in_dim(cells, odd * (planes - 1), 1, False)
    near_pairs = [(i, i ^ 1) for i in range(blocks)]
    early_pairs = [p for p in near_pairs if p[0] % DEPTH < DEPTH // 2 or p[1] % DEPTH == DEPTH - 1]
    across_pairs = [(i, (i + 1 if i % 2 else i - 1) % blocks) for i in range(blocks)]
    early_near = lax.ppermute(near_plane, "space", early_pairs)
    across = lax.ppermute(across_plane, "space", across_pairs)
    late_near = lax.ppermute(near_plane, "space", [p for p in near_pairs if p not in early_pairs])
    received = [x.reshape(species * rows, width) for x in (early_near, across, late_near)]
    mixing_row = lax.dynamic_index_in_dim(mixing, field, 1, False)
    reactions = rates.shape[0]
    pieces, *tables = pl.pallas_call(
        local_kernel,
        out_shape=(
            shape(rows, data + 8, width),
            jax.ShapeDtypeStruct((reactions, 3 * species), BF16),
            jax.ShapeDtypeStruct((species, 3 * species), BF16),
            jax.ShapeDtypeStruct((species, 3 * species), BF16),
            jax.ShapeDtypeStruct((species, 2 * reactions), BF16),
        ),
        in_specs=[SMEM] + [VMEM] * 6,
        out_specs=[VMEM] * 5,
        scratch_shapes=[pltpu.VMEM((data * rows, width), F32), pltpu.VMEM((planes * rows, width), F32)],
        compiler_params=LIMIT,
        name="local",
    )(block.reshape(1), cells, diffusivity, velocity, burn_tile[0], stoich, rates[None])
    pieces = pl.pallas_call(
        halo_kernel,
        out_shape=shape(rows, data + 8, width),
        in_specs=[SMEM] * 2 + [VMEM] * 6,
        out_specs=VMEM,
        input_output_aliases={2: 0},
        compiler_params=LIMIT,
        name="halo",
    )(odd.reshape(1), late.reshape(1), pieces, *received, diffusivity, velocity)
    pieces, tables, mixing_row = lax.optimization_barrier((pieces, tables, mixing_row))
    pieces = lax.all_to_all(pieces, "field", 0, 0, tiled=True)
    pieces = pl.pallas_call(
        react_kernel,
        out_shape=shape(fields, data, width),
        in_specs=[VMEM] * 6,
        out_specs=VMEM,
        scratch_shapes=[pltpu.SMEM((fields * planes + 1,), jnp.int32)],
        compiler_params=LIMIT,
        name="react",
    )(pieces, mixing_row, *tables)
    pieces = lax.all_to_all(pieces, "field", 0, 0, tiled=True)
    updated = pl.pallas_call(
        home_kernel,
        out_shape=shape(data * rows, width),
        in_specs=[VMEM],
        out_specs=pl.BlockSpec(memory_space=pltpu.HBM),
        scratch_shapes=[pltpu.VMEM((data * rows, width), F32), pltpu.SemaphoreType.DMA((4,))],
        compiler_params=LIMIT,
        name="home",
    )(pieces)
    return updated.reshape(1, species, planes, rows, width)


def solution(mesh):
    return jax.shard_map(
        per_device,
        mesh=mesh,
        in_specs=(
            P("field", None, "space", None, None),
            P("space", None, None),
            P("space", None, None),
            P("space", None, None),
            P(),
            P(),
            P("field", None, None),
            P("field", None, None),
        ),
        out_specs=P("field", None, "space", None, None),
        check_vma=False,
    )
```

```python
import jax
import jax.numpy as jnp
from jax import lax
from jax.experimental import pallas as pl
from jax.experimental.pallas import tpu as pltpu
from jax.sharding import PartitionSpec as P


NSUB = 4
LANES = 128
GROUPS = 10, 12
DEPTH = 16
F32 = jnp.float32
BF16 = jnp.bfloat16
VMEM = pl.BlockSpec(memory_space=pltpu.VMEM)
SMEM = pl.BlockSpec(memory_space=pltpu.SMEM)
LIMIT = pltpu.CompilerParams(vmem_limit_bytes=24 << 20)


def shape(*dims):
    return jax.ShapeDtypeStruct(dims, F32)


def local_kernel(
    block_ref, cells_ref, dif_ref, vel_ref, burn_ref, stoich_ref, rates_ref,
    out_ref, pairs_ref, partner_ref, squares_ref, produced_ref, rows_ref, flags_ref,
):
    species, planes, rows, _ = cells_ref.shape
    reaction_tables(stoich_ref, rates_ref, pairs_ref, partner_ref, squares_ref, produced_ref, species)
    tiles = planes * rows
    listed = burn_ref[pl.ds(block_ref[0], 1), :]
    match = lax.broadcasted_iota(jnp.int32, (tiles, listed.shape[1]), 0) == listed
    burning = jnp.max(jnp.where(match, 1.0, 0.0), axis=1, keepdims=True)
    flags_ref[...] = jnp.broadcast_to(burning, flags_ref.shape)
    last = planes - 1
    dif = [dif_ref[z] for z in range(planes)]
    vel = [vel_ref[z] for z in range(planes)]

    def one_species(s, carry):
        cells = [cells_ref[s, z] for z in range(planes)]
        for z in range(planes):
            center = cells[z]
            around = (
                pltpu.roll(center, 1, 1)
                + pltpu.roll(center, LANES - 1, 1)
                + pltpu.roll(center, 1, 0)
                + pltpu.roll(center, rows - 1, 0)
                - 6.0 * center
            )
            if z > 0:
                around = around + cells[z - 1]
            if z < last:
                around = around + cells[z + 1]
            drift = cells[z - 1] - center if z > 0 else -center
            start = pl.multiple_of((s * planes + z) * rows, rows)
            rows_ref[pl.ds(start, rows), :] = center + dif[z] * around + vel[z] * drift
        return carry

    lax.fori_loop(0, species, one_species, 0, unroll=4)
    data = species * planes
    for y in range(rows):
        out_ref[y, 0:data, :] = rows_ref[pl.ds(y, data, stride=rows), :]
        out_ref[y, data : data + 8, :] = jnp.zeros((8, LANES), F32)
        out_ref[y, data : data + planes, :] = flags_ref[pl.ds(y, planes, stride=rows), :]


def halo_kernel(
    odd_ref, late_ref, pieces_ref, early_near_ref, across_ref, late_near_ref, dif_ref, vel_ref, out_ref, full_ref, sems
):
    planes, rows, _ = dif_ref.shape
    species = across_ref.shape[0] // rows
    low = dif_ref[0] + vel_ref[0]
    high = dif_ref[planes - 1]
    steps = sems.shape[0]
    part = rows // steps

    def copy_of(step):
        at = pl.ds(step * part, part)
        return pltpu.make_async_copy(full_ref.at[at], out_ref.at[at], sems.at[step])

    odd, late = odd_ref[0] == 1, late_ref[0] == 1
    bottom, top = pl.ds(0, species, stride=planes), pl.ds(planes - 1, species, stride=planes)
    for y in range(rows):
        at = pl.ds(y, species, stride=rows)
        near = jnp.where(late, late_near_ref[at, :], early_near_ref[at, :])
        across = across_ref[at, :]
        below, above = jnp.where(odd, near, across), jnp.where(odd, across, near)
        full_ref[y, bottom, :] = pieces_ref[y, bottom, :] + low[y : y + 1] * below
        full_ref[y, top, :] = pieces_ref[y, top, :] + high[y : y + 1] * above
        full_ref[y, species * planes :, :] = pieces_ref[y, species * planes :, :]
        if y % part == part - 1:
            copy_of(y // part).start()
    for step in range(steps):
        copy_of(step).wait()


def in_parts(x):
    high = x.astype(BF16)
    return high, (x - high.astype(F32)).astype(BF16)


def factors(x):
    high, low = in_parts(x)
    return jnp.concatenate([high, low, high], 0)


def weights(w):
    high, low = in_parts(w)
    return jnp.concatenate([high, high, low], 1)


def dot(a, b):
    return jnp.dot(a, b, preferred_element_type=F32)


def chemistry(concent, pairs, partner, squares, produced):
    substep = 1.0 / NSUB
    for _ in range(NSUB):
        current = factors(concent)
        pair = dot(pairs, current)
        making = dot(produced, jnp.concatenate(in_parts(pair * pair), 0)) - dot(squares, factors(concent * concent))
        concent = (concent + substep * making) / (1.0 + substep * dot(partner, current))
    return concent


def react_kernel(in_ref, mix_ref, pairs_ref, partner_ref, squares_ref, produced_ref, out_ref, list_ref):
    fields, data, _ = out_ref.shape
    planes = mix_ref.shape[0]
    species = data // planes
    even = lax.broadcasted_iota(jnp.int32, (8, LANES), 0) % planes == 0
    mixing = jnp.where(even, mix_ref[0:1, :], mix_ref[1:2, :])

    def one_block(block, carry):
        at = pl.ds(pl.multiple_of(block * 8, 8), 8)
        cells = [in_ref[f, at, :] for f in range(fields)]
        total = cells[0]
        for f in range(1, fields):
            total = total + cells[f]
        ensemble = total * (1.0 / fields)
        for f in range(fields):
            out_ref[f, at, :] = cells[f] - mixing * (cells[f] - ensemble)
        return carry

    lax.fori_loop(0, data // 8, one_block, 0)
    marks = jnp.zeros((8, LANES), F32)
    for f in range(fields):
        marks = marks + in_ref[f, data : data + 8, :] * float(2**f)
    code = [jnp.max(marks[z : z + 1, :]).astype(jnp.int32) for z in range(planes)]
    count = jnp.int32(0)
    for z in range(planes):
        for f in range(fields):
            list_ref[count] = f * planes + z
            count = count + ((code[z] >> f) & 1)
    tables = [ref[...] for ref in (pairs_ref, partner_ref, squares_ref, produced_ref)]

    def react(size):
        @pl.loop(0, pl.cdiv(count, size))
        def _(group):
            first = group * size
            entries = [list_ref[jnp.minimum(first + j, count - 1)] for j in range(size)]
            places = [(lax.div(e, planes), lax.rem(e, planes)) for e in entries]
            concent = jnp.concatenate([out_ref[f, pl.ds(z, species, stride=planes), :] for f, z in places], 1)
            concent = chemistry(concent, *tables)
            for j, (f, z) in enumerate(places):

                @pl.when(first + j < count)
                def _():
                    out_ref[f, pl.ds(z, species, stride=planes), :] = concent[:, j * LANES : (j + 1) * LANES]

    small, large = GROUPS

    @pl.when(count <= small)
    def _():
        react(small)

    @pl.when(count > small)
    def _():
        react(large)


def home_kernel(in_ref, out_ref, rows_ref, sems):
    pieces, data, _ = in_ref.shape
    steps = sems.shape[0]
    part = data // steps
    copies = []
    for step in range(steps):
        size = part * pieces
        for y in range(pieces):
            at = pl.ds(step * size + y, part, stride=pieces)
            rows_ref[at, :] = in_ref[y, step * part : (step + 1) * part, :]
        at = pl.ds(step * size, size)
        copies.append(pltpu.make_async_copy(rows_ref.at[at], out_ref.at[at], sems.at[step]))
        copies[-1].start()
    for copy in copies:
        copy.wait()


def reaction_tables(stoich_ref, rates_ref, pairs_ref, partner_ref, squares_ref, produced_ref, species):
    rates = rates_ref[...]
    each = lax.broadcasted_iota(jnp.int32, (species, rates.shape[1]), 0)
    one, two, three, four = [jnp.where(each == stoich_ref[i : i + 1, :], 1.0, 0.0) for i in range(4)]
    both, produced = one + two, three + four
    along = (((1,), (1,)), ((), ()))
    highest = lax.Precision.HIGHEST
    scaled = rates * both
    partner = lax.dot_general(rates * one, two, along, highest, F32) + lax.dot_general(rates * two, one, along, highest, F32)
    squares = lax.dot_general(produced, 0.5 * scaled, along, highest, F32)
    pairs = jnp.sqrt(rates) * both
    high = pairs.astype(BF16).astype(F32)
    pairs_ref[...] = jnp.concatenate([high, high, pairs - high], 0).T.astype(BF16)
    partner_ref[...] = weights(partner)
    squares_ref[...] = weights(squares)
    half = (0.5 * produced).astype(BF16)
    produced_ref[...] = jnp.concatenate([half, half], 1)


def per_device(scalars, diffusivity, velocity, mixing, rates, stoich, burn_tile, helper_slot):
    block = lax.axis_index("space")
    blocks = lax.axis_size("space")
    fields = lax.axis_size("field")
    cells = scalars[0]
    species, planes, rows, width = cells.shape
    data = species * planes
    field = lax.axis_index("field")
    odd = block % 2
    late = (block % DEPTH) // (DEPTH // 2)
    near_plane = lax.dynamic_index_in_dim(cells, (1 - odd) * (planes - 1), 1, False)
    across_plane = lax.dynamic_index_in_dim(cells, odd * (planes - 1), 1, False)
    near_pairs = [(i, i ^ 1) for i in range(blocks)]
    half = [i % DEPTH < DEPTH // 2 for i in range(blocks)]
    across_pairs = [(i, (i + 1 if i % 2 else i - 1) % blocks) for i in range(blocks)]
    early_near = lax.ppermute(near_plane, "space", [p for p in near_pairs if half[p[0]]])
    across = lax.ppermute(across_plane, "space", across_pairs)
    late_near = lax.ppermute(near_plane, "space", [p for p in near_pairs if not half[p[0]]])
    received = [x.reshape(species * rows, width) for x in (early_near, across, late_near)]
    reactions = rates.shape[0]
    pieces, *tables = pl.pallas_call(
        local_kernel,
        out_shape=(
            shape(rows, data + 8, width),
            jax.ShapeDtypeStruct((reactions, 3 * species), BF16),
            jax.ShapeDtypeStruct((species, 3 * species), BF16),
            jax.ShapeDtypeStruct((species, 3 * species), BF16),
            jax.ShapeDtypeStruct((species, 2 * reactions), BF16),
        ),
        in_specs=[SMEM] + [VMEM] * 6,
        out_specs=[VMEM] * 5,
        scratch_shapes=[pltpu.VMEM((data * rows, width), F32), pltpu.VMEM((planes * rows, width), F32)],
        compiler_params=LIMIT,
        name="local",
    )(block.reshape(1), cells, diffusivity, velocity, burn_tile[0], stoich, rates[None])
    pieces = pltpu.with_memory_space_constraint(pieces, pltpu.VMEM)
    pieces = pl.pallas_call(
        halo_kernel,
        out_shape=shape(rows, data + 8, width),
        in_specs=[SMEM] * 2 + [VMEM] * 6,
        out_specs=pl.BlockSpec(memory_space=pltpu.HBM),
        scratch_shapes=[pltpu.VMEM((rows, data + 8, width), F32), pltpu.SemaphoreType.DMA((4,))],
        compiler_params=LIMIT,
        name="halo",
    )(odd.reshape(1), late.reshape(1), pieces, *received, diffusivity, velocity)
    pieces, mixing = lax.optimization_barrier((pieces, mixing))
    mixing_row = lax.dynamic_index_in_dim(mixing, field, 1, False)
    pieces = lax.all_to_all(pieces, "field", 0, 0, tiled=True)
    pieces = pl.pallas_call(
        react_kernel,
        out_shape=shape(fields, data, width),
        in_specs=[VMEM] * 6,
        out_specs=VMEM,
        scratch_shapes=[pltpu.SMEM((fields * planes + 1,), jnp.int32)],
        compiler_params=LIMIT,
        name="react",
    )(pieces, mixing_row, *tables)
    pieces = lax.all_to_all(pieces, "field", 0, 0, tiled=True)
    updated = pl.pallas_call(
        home_kernel,
        out_shape=shape(data * rows, width),
        in_specs=[VMEM],
        out_specs=pl.BlockSpec(memory_space=pltpu.HBM),
        scratch_shapes=[pltpu.VMEM((data * rows, width), F32), pltpu.SemaphoreType.DMA((4,))],
        compiler_params=LIMIT,
        name="home",
    )(pieces)
    return updated.reshape(1, species, planes, rows, width)


def solution(mesh):
    return jax.shard_map(
        per_device,
        mesh=mesh,
        in_specs=(
            P("field", None, "space", None, None),
            P("space", None, None),
            P("space", None, None),
            P("space", None, None),
            P(),
            P(),
            P("field", None, None),
            P("field", None, None),
        ),
        out_specs=P("field", None, "space", None, None),
        check_vma=False,
    )
```

```python
import jax
import jax.numpy as jnp
from jax import lax
from jax.experimental import pallas as pl
from jax.experimental.pallas import tpu as pltpu
from jax.sharding import PartitionSpec as P


NSUB = 4
LANES = 128
GROUPS = 10, 12
DEPTH = 16
ORDER = (13, 1, 8, 3, 6, 10, 9, 5, 14, 15, 11, 0, 4, 12, 7, 2)
F32 = jnp.float32
BF16 = jnp.bfloat16
VMEM = pl.BlockSpec(memory_space=pltpu.VMEM)
SMEM = pl.BlockSpec(memory_space=pltpu.SMEM)
LIMIT = pltpu.CompilerParams(vmem_limit_bytes=24 << 20)


def shape(*dims):
    return jax.ShapeDtypeStruct(dims, F32)


def local_kernel(
    block_ref, cells_ref, dif_ref, vel_ref, burn_ref, stoich_ref, rates_ref,
    out_ref, pairs_ref, partner_ref, squares_ref, produced_ref, rows_ref, flags_ref,
):
    species, planes, rows, _ = cells_ref.shape
    reaction_tables(stoich_ref, rates_ref, pairs_ref, partner_ref, squares_ref, produced_ref, species)
    tiles = planes * rows
    listed = burn_ref[pl.ds(block_ref[0], 1), :]
    match = lax.broadcasted_iota(jnp.int32, (tiles, listed.shape[1]), 0) == listed
    burning = jnp.max(jnp.where(match, 1.0, 0.0), axis=1, keepdims=True)
    flags_ref[...] = jnp.broadcast_to(burning, flags_ref.shape)
    last = planes - 1
    dif = [dif_ref[z] for z in range(planes)]
    vel = [vel_ref[z] for z in range(planes)]

    def one_species(s, carry):
        cells = [cells_ref[s, z] for z in range(planes)]
        for z in range(planes):
            center = cells[z]
            around = (
                pltpu.roll(center, 1, 1)
                + pltpu.roll(center, LANES - 1, 1)
                + pltpu.roll(center, 1, 0)
                + pltpu.roll(center, rows - 1, 0)
                - 6.0 * center
            )
            if z > 0:
                around = around + cells[z - 1]
            if z < last:
                around = around + cells[z + 1]
            drift = cells[z - 1] - center if z > 0 else -center
            start = pl.multiple_of((s * planes + z) * rows, rows)
            rows_ref[pl.ds(start, rows), :] = center + dif[z] * around + vel[z] * drift
        return carry

    lax.fori_loop(0, species, one_species, 0, unroll=4)
    data = species * planes
    for y in range(rows):
        out_ref[y, 0:data, :] = rows_ref[pl.ds(y, data, stride=rows), :]
        out_ref[y, data : data + 8, :] = jnp.zeros((8, LANES), F32)
        out_ref[y, data : data + planes, :] = flags_ref[pl.ds(y, planes, stride=rows), :]


def halo_kernel(odd_ref, late_ref, pieces_ref, early_near_ref, across_ref, late_near_ref, dif_ref, vel_ref, out_ref):
    planes, rows, _ = dif_ref.shape
    species = across_ref.shape[0] // rows
    low = dif_ref[0] + vel_ref[0]
    high = dif_ref[planes - 1]

    def add(below_ref, above_ref):
        for y in range(rows):
            at = pl.ds(y, species, stride=rows)
            bottom, top = pl.ds(0, species, stride=planes), pl.ds(planes - 1, species, stride=planes)
            out_ref[y, bottom, :] = pieces_ref[y, bottom, :] + low[y : y + 1] * below_ref[at, :]
            out_ref[y, top, :] = pieces_ref[y, top, :] + high[y : y + 1] * above_ref[at, :]
            out_ref[y, species * planes :, :] = pieces_ref[y, species * planes :, :]

    for late, near_ref in enumerate((early_near_ref, late_near_ref)):

        @pl.when((odd_ref[0] == 0) & (late_ref[0] == late))
        def _():
            add(across_ref, near_ref)

        @pl.when((odd_ref[0] == 1) & (late_ref[0] == late))
        def _():
            add(near_ref, across_ref)


def in_parts(x):
    high = x.astype(BF16)
    return high, (x - high.astype(F32)).astype(BF16)


def factors(x):
    high, low = in_parts(x)
    return jnp.concatenate([high, low, high], 0)


def weights(w):
    high, low = in_parts(w)
    return jnp.concatenate([high, high, low], 1)


def dot(a, b):
    return jnp.dot(a, b, preferred_element_type=F32)


def chemistry(concent, pairs, partner, squares, produced):
    substep = 1.0 / NSUB
    for _ in range(NSUB):
        current = factors(concent)
        pair = dot(pairs, current)
        making = dot(produced, jnp.concatenate(in_parts(pair * pair), 0)) - dot(squares, factors(concent * concent))
        concent = (concent + substep * making) / (1.0 + substep * dot(partner, current))
    return concent


def react_kernel(in_ref, mix_ref, pairs_ref, partner_ref, squares_ref, produced_ref, out_ref, list_ref):
    fields, data, _ = out_ref.shape
    planes = mix_ref.shape[0]
    species = data // planes
    even = lax.broadcasted_iota(jnp.int32, (8, LANES), 0) % planes == 0
    mixing = jnp.where(even, mix_ref[0:1, :], mix_ref[1:2, :])

    def one_block(block, carry):
        at = pl.ds(pl.multiple_of(block * 8, 8), 8)
        cells = [in_ref[f, at, :] for f in range(fields)]
        total = cells[0]
        for f in range(1, fields):
            total = total + cells[f]
        ensemble = total * (1.0 / fields)
        for f in range(fields):
            out_ref[f, at, :] = cells[f] - mixing * (cells[f] - ensemble)
        return carry

    lax.fori_loop(0, data // 8, one_block, 0)
    marks = jnp.zeros((8, LANES), F32)
    for f in range(fields):
        marks = marks + in_ref[f, data : data + 8, :] * float(2**f)
    code = [jnp.max(marks[z : z + 1, :]).astype(jnp.int32) for z in range(planes)]
    count = jnp.int32(0)
    for z in range(planes):
        for f in range(fields):
            list_ref[count] = f * planes + z
            count = count + ((code[z] >> f) & 1)
    tables = [ref[...] for ref in (pairs_ref, partner_ref, squares_ref, produced_ref)]

    def react(size):
        @pl.loop(0, pl.cdiv(count, size))
        def _(group):
            first = group * size
            entries = [list_ref[jnp.minimum(first + j, count - 1)] for j in range(size)]
            places = [(lax.div(e, planes), lax.rem(e, planes)) for e in entries]
            concent = jnp.concatenate([out_ref[f, pl.ds(z, species, stride=planes), :] for f, z in places], 1)
            concent = chemistry(concent, *tables)
            for j, (f, z) in enumerate(places):

                @pl.when(first + j < count)
                def _():
                    out_ref[f, pl.ds(z, species, stride=planes), :] = concent[:, j * LANES : (j + 1) * LANES]

    small, large = GROUPS

    @pl.when(count <= small)
    def _():
        react(small)

    @pl.when(count > small)
    def _():
        react(large)


def home_kernel(in_ref, out_ref, rows_ref, sems):
    pieces, data, _ = in_ref.shape
    steps = sems.shape[0]
    part = data // steps
    copies = []
    for step in range(steps):
        size = part * pieces
        for y in range(pieces):
            at = pl.ds(step * size + y, part, stride=pieces)
            rows_ref[at, :] = in_ref[y, step * part : (step + 1) * part, :]
        at = pl.ds(step * size, size)
        copies.append(pltpu.make_async_copy(rows_ref.at[at], out_ref.at[at], sems.at[step]))
        copies[-1].start()
    for copy in copies:
        copy.wait()


def reaction_tables(stoich_ref, rates_ref, pairs_ref, partner_ref, squares_ref, produced_ref, species):
    rates = rates_ref[...]
    each = lax.broadcasted_iota(jnp.int32, (species, rates.shape[1]), 0)
    one, two, three, four = [jnp.where(each == stoich_ref[i : i + 1, :], 1.0, 0.0) for i in range(4)]
    both, produced = one + two, three + four
    along = (((1,), (1,)), ((), ()))
    highest = lax.Precision.HIGHEST
    scaled = rates * both
    partner = lax.dot_general(rates * one, two, along, highest, F32) + lax.dot_general(rates * two, one, along, highest, F32)
    squares = lax.dot_general(produced, 0.5 * scaled, along, highest, F32)
    pairs = jnp.sqrt(rates) * both
    high = pairs.astype(BF16).astype(F32)
    pairs_ref[...] = jnp.concatenate([high, high, pairs - high], 0).T.astype(BF16)
    partner_ref[...] = weights(partner)
    squares_ref[...] = weights(squares)
    half = (0.5 * produced).astype(BF16)
    produced_ref[...] = jnp.concatenate([half, half], 1)


def per_device(scalars, diffusivity, velocity, mixing, rates, stoich, burn_tile, helper_slot):
    block = lax.axis_index("space")
    blocks = lax.axis_size("space")
    fields = lax.axis_size("field")
    cells = scalars[0]
    species, planes, rows, width = cells.shape
    data = species * planes
    field = lax.axis_index("field")
    odd = block % 2
    late = (block % DEPTH) // (DEPTH // 2)
    near_plane = lax.dynamic_index_in_dim(cells, (1 - odd) * (planes - 1), 1, False)
    across_plane = lax.dynamic_index_in_dim(cells, odd * (planes - 1), 1, False)
    near_pairs = [(i, i ^ 1) for i in range(blocks)]
    half = [i % DEPTH < DEPTH // 2 for i in range(blocks)]
    across_pairs = [(i, (i + 1 if i % 2 else i - 1) % blocks) for i in range(blocks)]
    early_near = lax.ppermute(near_plane, "space", [p for p in near_pairs if half[p[0]]])
    across = lax.ppermute(across_plane, "space", across_pairs)
    late_near = lax.ppermute(near_plane, "space", [p for p in near_pairs if not half[p[0]]])
    received = [x.reshape(species * rows, width) for x in (early_near, across, late_near)]
    owned = sum(jnp.where(field == member, place, 0) for place, member in enumerate(ORDER))
    mixing_row = lax.dynamic_index_in_dim(mixing, owned, 1, False)
    reactions = rates.shape[0]
    pieces, *tables = pl.pallas_call(
        local_kernel,
        out_shape=(
            shape(rows, data + 8, width),
            jax.ShapeDtypeStruct((reactions, 3 * species), BF16),
            jax.ShapeDtypeStruct((species, 3 * species), BF16),
            jax.ShapeDtypeStruct((species, 3 * species), BF16),
            jax.ShapeDtypeStruct((species, 2 * reactions), BF16),
        ),
        in_specs=[SMEM] + [VMEM] * 6,
        out_specs=[VMEM] * 5,
        scratch_shapes=[pltpu.VMEM((data * rows, width), F32), pltpu.VMEM((planes * rows, width), F32)],
        compiler_params=LIMIT,
        name="local",
    )(block.reshape(1), cells, diffusivity, velocity, burn_tile[0], stoich, rates[None])
    pieces = pl.pallas_call(
        halo_kernel,
        out_shape=shape(rows, data + 8, width),
        in_specs=[SMEM] * 2 + [VMEM] * 6,
        out_specs=VMEM,
        input_output_aliases={2: 0},
        compiler_params=LIMIT,
        name="halo",
    )(odd.reshape(1), late.reshape(1), pieces, *received, diffusivity, velocity)
    pieces, tables, mixing_row = lax.optimization_barrier((pieces, tables, mixing_row))
    pieces = lax.all_to_all(pieces, "field", 0, 0, axis_index_groups=[list(ORDER)], tiled=True)
    pieces = pl.pallas_call(
        react_kernel,
        out_shape=shape(fields, data, width),
        in_specs=[VMEM] * 6,
        out_specs=VMEM,
        scratch_shapes=[pltpu.SMEM((fields * planes + 1,), jnp.int32)],
        compiler_params=LIMIT,
        name="react",
    )(pieces, mixing_row, *tables)
    pieces = lax.all_to_all(pieces, "field", 0, 0, axis_index_groups=[list(ORDER)], tiled=True)
    updated = pl.pallas_call(
        home_kernel,
        out_shape=shape(data * rows, width),
        in_specs=[VMEM],
        out_specs=pl.BlockSpec(memory_space=pltpu.HBM),
        scratch_shapes=[pltpu.VMEM((data * rows, width), F32), pltpu.SemaphoreType.DMA((4,))],
        compiler_params=LIMIT,
        name="home",
    )(pieces)
    return updated.reshape(1, species, planes, rows, width)


def solution(mesh):
    return jax.shard_map(
        per_device,
        mesh=mesh,
        in_specs=(
            P("field", None, "space", None, None),
            P("space", None, None),
            P("space", None, None),
            P("space", None, None),
            P(),
            P(),
            P("field", None, None),
            P("field", None, None),
        ),
        out_specs=P("field", None, "space", None, None),
        check_vma=False,
    )
```

```python
import jax
import jax.numpy as jnp
from jax import lax
from jax.experimental import pallas as pl
from jax.experimental.pallas import tpu as pltpu
from jax.sharding import PartitionSpec as P


NSUB = 4
LANES = 128
GROUPS = 8, 10, 12
DEPTH = 16
ORDER = (13, 1, 8, 3, 6, 10, 9, 5, 14, 15, 11, 0, 4, 12, 7, 2)
F32 = jnp.float32
BF16 = jnp.bfloat16
VMEM = pl.BlockSpec(memory_space=pltpu.VMEM)
SMEM = pl.BlockSpec(memory_space=pltpu.SMEM)
LIMIT = pltpu.CompilerParams(vmem_limit_bytes=24 << 20)


def shape(*dims):
    return jax.ShapeDtypeStruct(dims, F32)


def local_kernel(
    block_ref, cells_ref, dif_ref, vel_ref, burn_ref, stoich_ref, rates_ref,
    out_ref, pairs_ref, partner_ref, squares_ref, produced_ref, rows_ref, flags_ref,
):
    species, planes, rows, _ = cells_ref.shape
    reaction_tables(stoich_ref, rates_ref, pairs_ref, partner_ref, squares_ref, produced_ref, species)
    tiles = planes * rows
    listed = burn_ref[pl.ds(block_ref[0], 1), :]
    match = lax.broadcasted_iota(jnp.int32, (tiles, listed.shape[1]), 0) == listed
    burning = jnp.max(jnp.where(match, 1.0, 0.0), axis=1, keepdims=True)
    flags_ref[...] = jnp.broadcast_to(burning, flags_ref.shape)
    last = planes - 1
    dif = [dif_ref[z] for z in range(planes)]
    vel = [vel_ref[z] for z in range(planes)]

    def one_species(s, carry):
        cells = [cells_ref[s, z] for z in range(planes)]
        for z in range(planes):
            center = cells[z]
            around = (
                pltpu.roll(center, 1, 1)
                + pltpu.roll(center, LANES - 1, 1)
                + pltpu.roll(center, 1, 0)
                + pltpu.roll(center, rows - 1, 0)
                - 6.0 * center
            )
            if z > 0:
                around = around + cells[z - 1]
            if z < last:
                around = around + cells[z + 1]
            drift = cells[z - 1] - center if z > 0 else -center
            start = pl.multiple_of((s * planes + z) * rows, rows)
            rows_ref[pl.ds(start, rows), :] = center + dif[z] * around + vel[z] * drift
        return carry

    lax.fori_loop(0, species, one_species, 0, unroll=4)
    data = species * planes
    for y in range(rows):
        out_ref[y, 0:data, :] = rows_ref[pl.ds(y, data, stride=rows), :]
        out_ref[y, data : data + 8, :] = jnp.zeros((8, LANES), F32)
        out_ref[y, data : data + planes, :] = flags_ref[pl.ds(y, planes, stride=rows), :]


def halo_kernel(odd_ref, late_ref, pieces_ref, early_near_ref, across_ref, late_near_ref, dif_ref, vel_ref, out_ref):
    planes, rows, _ = dif_ref.shape
    species = across_ref.shape[0] // rows
    low = dif_ref[0] + vel_ref[0]
    high = dif_ref[planes - 1]

    def add(below_ref, above_ref):
        for y in range(rows):
            at = pl.ds(y, species, stride=rows)
            bottom, top = pl.ds(0, species, stride=planes), pl.ds(planes - 1, species, stride=planes)
            out_ref[y, bottom, :] = pieces_ref[y, bottom, :] + low[y : y + 1] * below_ref[at, :]
            out_ref[y, top, :] = pieces_ref[y, top, :] + high[y : y + 1] * above_ref[at, :]
            out_ref[y, species * planes :, :] = pieces_ref[y, species * planes :, :]

    for late, near_ref in enumerate((early_near_ref, late_near_ref)):

        @pl.when((odd_ref[0] == 0) & (late_ref[0] == late))
        def _():
            add(across_ref, near_ref)

        @pl.when((odd_ref[0] == 1) & (late_ref[0] == late))
        def _():
            add(near_ref, across_ref)


def in_parts(x):
    high = x.astype(BF16)
    return high, (x - high.astype(F32)).astype(BF16)


def factors(x):
    high, low = in_parts(x)
    return jnp.concatenate([high, low, high], 0)


def weights(w):
    high, low = in_parts(w)
    return jnp.concatenate([high, high, low], 1)


def dot(a, b):
    return jnp.dot(a, b, preferred_element_type=F32)


def chemistry(concent, pairs, partner, squares, produced):
    substep = 1.0 / NSUB
    for _ in range(NSUB):
        current = factors(concent)
        pair = dot(pairs, current)
        making = dot(produced, jnp.concatenate(in_parts(pair * pair), 0)) - dot(squares, factors(concent * concent))
        concent = (concent + substep * making) / (1.0 + substep * dot(partner, current))
    return concent


def react_kernel(in_ref, mix_ref, pairs_ref, partner_ref, squares_ref, produced_ref, out_ref, list_ref):
    fields, data, _ = out_ref.shape
    planes = mix_ref.shape[0]
    species = data // planes
    even = lax.broadcasted_iota(jnp.int32, (8, LANES), 0) % planes == 0
    mixing = jnp.where(even, mix_ref[0:1, :], mix_ref[1:2, :])

    def one_block(block, carry):
        at = pl.ds(pl.multiple_of(block * 8, 8), 8)
        cells = [in_ref[f, at, :] for f in range(fields)]
        total = cells[0]
        for f in range(1, fields):
            total = total + cells[f]
        ensemble = total * (1.0 / fields)
        for f in range(fields):
            out_ref[f, at, :] = cells[f] - mixing * (cells[f] - ensemble)
        return carry

    lax.fori_loop(0, data // 8, one_block, 0)
    marks = jnp.zeros((8, LANES), F32)
    for f in range(fields):
        marks = marks + in_ref[f, data : data + 8, :] * float(2**f)
    code = [jnp.max(marks[z : z + 1, :]).astype(jnp.int32) for z in range(planes)]
    count = jnp.int32(0)
    for z in range(planes):
        for f in range(fields):
            list_ref[count] = f * planes + z
            count = count + ((code[z] >> f) & 1)
    tables = [ref[...] for ref in (pairs_ref, partner_ref, squares_ref, produced_ref)]

    def react(size):
        @pl.loop(0, pl.cdiv(count, size))
        def _(group):
            first = group * size
            entries = [list_ref[jnp.minimum(first + j, count - 1)] for j in range(size)]
            places = [(lax.div(e, planes), lax.rem(e, planes)) for e in entries]
            concent = jnp.concatenate([out_ref[f, pl.ds(z, species, stride=planes), :] for f, z in places], 1)
            concent = chemistry(concent, *tables)
            for j, (f, z) in enumerate(places):

                @pl.when(first + j < count)
                def _():
                    out_ref[f, pl.ds(z, species, stride=planes), :] = concent[:, j * LANES : (j + 1) * LANES]

    below = -1
    for size in GROUPS:
        fits = count > below
        if size != GROUPS[-1]:
            fits &= count <= size

        @pl.when(fits)
        def _():
            react(size)

        below = size


def home_kernel(in_ref, out_ref, rows_ref, sems):
    pieces, data, _ = in_ref.shape
    steps = sems.shape[0]
    part = data // steps
    copies = []
    for step in range(steps):
        size = part * pieces
        for y in range(pieces):
            at = pl.ds(step * size + y, part, stride=pieces)
            rows_ref[at, :] = in_ref[y, step * part : (step + 1) * part, :]
        at = pl.ds(step * size, size)
        copies.append(pltpu.make_async_copy(rows_ref.at[at], out_ref.at[at], sems.at[step]))
        copies[-1].start()
    for copy in copies:
        copy.wait()


def reaction_tables(stoich_ref, rates_ref, pairs_ref, partner_ref, squares_ref, produced_ref, species):
    rates = rates_ref[...]
    each = lax.broadcasted_iota(jnp.int32, (species, rates.shape[1]), 0)
    one, two, three, four = [jnp.where(each == stoich_ref[i : i + 1, :], 1.0, 0.0) for i in range(4)]
    both, produced = one + two, three + four
    along = (((1,), (1,)), ((), ()))
    highest = lax.Precision.HIGHEST
    scaled = rates * both
    partner = lax.dot_general(rates * one, two, along, highest, F32) + lax.dot_general(rates * two, one, along, highest, F32)
    squares = lax.dot_general(produced, 0.5 * scaled, along, highest, F32)
    pairs = jnp.sqrt(rates) * both
    high = pairs.astype(BF16).astype(F32)
    pairs_ref[...] = jnp.concatenate([high, high, pairs - high], 0).T.astype(BF16)
    partner_ref[...] = weights(partner)
    squares_ref[...] = weights(squares)
    half = (0.5 * produced).astype(BF16)
    produced_ref[...] = jnp.concatenate([half, half], 1)


def per_device(scalars, diffusivity, velocity, mixing, rates, stoich, burn_tile, helper_slot):
    block = lax.axis_index("space")
    blocks = lax.axis_size("space")
    fields = lax.axis_size("field")
    cells = scalars[0]
    species, planes, rows, width = cells.shape
    data = species * planes
    field = lax.axis_index("field")
    odd = block % 2
    late = (block % DEPTH) // (DEPTH // 2)
    near_plane = lax.dynamic_index_in_dim(cells, (1 - odd) * (planes - 1), 1, False)
    across_plane = lax.dynamic_index_in_dim(cells, odd * (planes - 1), 1, False)
    near_pairs = [(i, i ^ 1) for i in range(blocks)]
    half = [i % DEPTH < DEPTH // 2 for i in range(blocks)]
    across_pairs = [(i, (i + 1 if i % 2 else i - 1) % blocks) for i in range(blocks)]
    early_near = lax.ppermute(near_plane, "space", [p for p in near_pairs if half[p[0]]])
    across = lax.ppermute(across_plane, "space", across_pairs)
    late_near = lax.ppermute(near_plane, "space", [p for p in near_pairs if not half[p[0]]])
    received = [x.reshape(species * rows, width) for x in (early_near, across, late_near)]
    owned = sum(jnp.where(field == member, place, 0) for place, member in enumerate(ORDER))
    mixing_row = lax.dynamic_index_in_dim(mixing, owned, 1, False)
    reactions = rates.shape[0]
    pieces, *tables = pl.pallas_call(
        local_kernel,
        out_shape=(
            shape(rows, data + 8, width),
            jax.ShapeDtypeStruct((reactions, 3 * species), BF16),
            jax.ShapeDtypeStruct((species, 3 * species), BF16),
            jax.ShapeDtypeStruct((species, 3 * species), BF16),
            jax.ShapeDtypeStruct((species, 2 * reactions), BF16),
        ),
        in_specs=[SMEM] + [VMEM] * 6,
        out_specs=[VMEM] * 5,
        scratch_shapes=[pltpu.VMEM((data * rows, width), F32), pltpu.VMEM((planes * rows, width), F32)],
        compiler_params=LIMIT,
        name="local",
    )(block.reshape(1), cells, diffusivity, velocity, burn_tile[0], stoich, rates[None])
    pieces = pl.pallas_call(
        halo_kernel,
        out_shape=shape(rows, data + 8, width),
        in_specs=[SMEM] * 2 + [VMEM] * 6,
        out_specs=VMEM,
        input_output_aliases={2: 0},
        compiler_params=LIMIT,
        name="halo",
    )(odd.reshape(1), late.reshape(1), pieces, *received, diffusivity, velocity)
    pieces, tables, mixing_row = lax.optimization_barrier((pieces, tables, mixing_row))
    pieces = lax.all_to_all(pieces, "field", 0, 0, axis_index_groups=[list(ORDER)], tiled=True)
    pieces = pl.pallas_call(
        react_kernel,
        out_shape=shape(fields, data, width),
        in_specs=[VMEM] * 6,
        out_specs=VMEM,
        scratch_shapes=[pltpu.SMEM((fields * planes + 1,), jnp.int32)],
        compiler_params=LIMIT,
        name="react",
    )(pieces, mixing_row, *tables)
    pieces = lax.all_to_all(pieces, "field", 0, 0, axis_index_groups=[list(ORDER)], tiled=True)
    updated = pl.pallas_call(
        home_kernel,
        out_shape=shape(data * rows, width),
        in_specs=[VMEM],
        out_specs=pl.BlockSpec(memory_space=pltpu.HBM),
        scratch_shapes=[pltpu.VMEM((data * rows, width), F32), pltpu.SemaphoreType.DMA((8,))],
        compiler_params=LIMIT,
        name="home",
    )(pieces)
    return updated.reshape(1, species, planes, rows, width)


def solution(mesh):
    return jax.shard_map(
        per_device,
        mesh=mesh,
        in_specs=(
            P("field", None, "space", None, None),
            P("space", None, None),
            P("space", None, None),
            P("space", None, None),
            P(),
            P(),
            P("field", None, None),
            P("field", None, None),
        ),
        out_specs=P("field", None, "space", None, None),
        check_vma=False,
    )
```

```python
import jax
import jax.numpy as jnp
from jax import lax
from jax.experimental import pallas as pl
from jax.experimental.pallas import tpu as pltpu
from jax.sharding import PartitionSpec as P


NSUB = 4
LANES = 128
GROUPS = 8, 10, 12
DEPTH = 16
ORDER = (13, 1, 8, 3, 6, 10, 9, 5, 14, 15, 11, 0, 4, 12, 7, 2)
F32 = jnp.float32
BF16 = jnp.bfloat16
VMEM = pl.BlockSpec(memory_space=pltpu.VMEM)
SMEM = pl.BlockSpec(memory_space=pltpu.SMEM)
LIMIT = pltpu.CompilerParams(vmem_limit_bytes=24 << 20)


def shape(*dims):
    return jax.ShapeDtypeStruct(dims, F32)


def local_kernel(
    block_ref, cells_ref, dif_ref, vel_ref, burn_ref, stoich_ref, rates_ref,
    out_ref, pairs_ref, partner_ref, squares_ref, produced_ref, rows_ref, flags_ref,
):
    species, planes, rows, _ = cells_ref.shape
    reaction_tables(stoich_ref, rates_ref, pairs_ref, partner_ref, squares_ref, produced_ref, species)
    tiles = planes * rows
    listed = burn_ref[pl.ds(block_ref[0], 1), :]
    match = lax.broadcasted_iota(jnp.int32, (tiles, listed.shape[1]), 0) == listed
    burning = jnp.max(jnp.where(match, 1.0, 0.0), axis=1, keepdims=True)
    flags_ref[...] = jnp.broadcast_to(burning, flags_ref.shape)
    last = planes - 1
    dif = [dif_ref[z] for z in range(planes)]
    vel = [vel_ref[z] for z in range(planes)]

    def one_species(s, carry):
        cells = [cells_ref[s, z] for z in range(planes)]
        for z in range(planes):
            center = cells[z]
            around = (
                pltpu.roll(center, 1, 1)
                + pltpu.roll(center, LANES - 1, 1)
                + pltpu.roll(center, 1, 0)
                + pltpu.roll(center, rows - 1, 0)
                - 6.0 * center
            )
            if z > 0:
                around = around + cells[z - 1]
            if z < last:
                around = around + cells[z + 1]
            drift = cells[z - 1] - center if z > 0 else -center
            start = pl.multiple_of((s * planes + z) * rows, rows)
            rows_ref[pl.ds(start, rows), :] = center + dif[z] * around + vel[z] * drift
        return carry

    lax.fori_loop(0, species, one_species, 0, unroll=4)
    data = species * planes
    for y in range(rows):
        out_ref[y, 0:data, :] = rows_ref[pl.ds(y, data, stride=rows), :]
        out_ref[y, data : data + 8, :] = jnp.zeros((8, LANES), F32)
        out_ref[y, data : data + planes, :] = flags_ref[pl.ds(y, planes, stride=rows), :]


def halo_kernel(odd_ref, late_ref, pieces_ref, early_near_ref, across_ref, late_near_ref, dif_ref, vel_ref, out_ref):
    planes, rows, _ = dif_ref.shape
    species = across_ref.shape[0] // rows
    low = dif_ref[0] + vel_ref[0]
    high = dif_ref[planes - 1]

    def add(below_ref, above_ref):
        for y in range(rows):
            at = pl.ds(y, species, stride=rows)
            bottom, top = pl.ds(0, species, stride=planes), pl.ds(planes - 1, species, stride=planes)
            out_ref[y, bottom, :] = pieces_ref[y, bottom, :] + low[y : y + 1] * below_ref[at, :]
            out_ref[y, top, :] = pieces_ref[y, top, :] + high[y : y + 1] * above_ref[at, :]
            out_ref[y, species * planes :, :] = pieces_ref[y, species * planes :, :]

    for late, near_ref in enumerate((early_near_ref, late_near_ref)):

        @pl.when((odd_ref[0] == 0) & (late_ref[0] == late))
        def _():
            add(across_ref, near_ref)

        @pl.when((odd_ref[0] == 1) & (late_ref[0] == late))
        def _():
            add(near_ref, across_ref)


def in_parts(x):
    high = x.astype(BF16)
    return high, (x - high.astype(F32)).astype(BF16)


def factors(x):
    high, low = in_parts(x)
    return jnp.concatenate([high, low, high], 0)


def weights(w):
    high, low = in_parts(w)
    return jnp.concatenate([high, high, low], 1)


def dot(a, b):
    return jnp.dot(a, b, preferred_element_type=F32)


def chemistry(concent, pairs, partner, squares, produced):
    substep = 1.0 / NSUB
    species = concent.shape[0]
    both = jnp.concatenate([partner, pairs], 0)
    made = jnp.concatenate([produced, -squares], 1)
    for _ in range(NSUB):
        picked = dot(both, factors(concent))
        pair = picked[species:]
        making = dot(made, jnp.concatenate([*in_parts(pair * pair), factors(concent * concent)], 0))
        concent = (concent + substep * making) / (1.0 + substep * picked[:species])
    return concent


def react_kernel(in_ref, mix_ref, pairs_ref, partner_ref, squares_ref, produced_ref, out_ref, list_ref):
    fields, data, _ = out_ref.shape
    planes = mix_ref.shape[0]
    species = data // planes
    even = lax.broadcasted_iota(jnp.int32, (8, LANES), 0) % planes == 0
    mixing = jnp.where(even, mix_ref[0:1, :], mix_ref[1:2, :])

    def one_block(block, carry):
        at = pl.ds(pl.multiple_of(block * 8, 8), 8)
        cells = [in_ref[f, at, :] for f in range(fields)]
        total = cells[0]
        for f in range(1, fields):
            total = total + cells[f]
        ensemble = total * (1.0 / fields)
        for f in range(fields):
            out_ref[f, at, :] = cells[f] - mixing * (cells[f] - ensemble)
        return carry

    lax.fori_loop(0, data // 8, one_block, 0)
    marks = jnp.zeros((8, LANES), F32)
    for f in range(fields):
        marks = marks + in_ref[f, data : data + 8, :] * float(2**f)
    code = [jnp.max(marks[z : z + 1, :]).astype(jnp.int32) for z in range(planes)]
    count = jnp.int32(0)
    for z in range(planes):
        for f in range(fields):
            list_ref[count] = f * planes + z
            count = count + ((code[z] >> f) & 1)
    tables = [ref[...] for ref in (pairs_ref, partner_ref, squares_ref, produced_ref)]

    def react(size):
        @pl.loop(0, pl.cdiv(count, size))
        def _(group):
            first = group * size
            entries = [list_ref[jnp.minimum(first + j, count - 1)] for j in range(size)]
            places = [(lax.div(e, planes), lax.rem(e, planes)) for e in entries]
            concent = jnp.concatenate([out_ref[f, pl.ds(z, species, stride=planes), :] for f, z in places], 1)
            concent = chemistry(concent, *tables)
            for j, (f, z) in enumerate(places):

                @pl.when(first + j < count)
                def _():
                    out_ref[f, pl.ds(z, species, stride=planes), :] = concent[:, j * LANES : (j + 1) * LANES]

    below = -1
    for size in GROUPS:
        fits = count > below
        if size != GROUPS[-1]:
            fits &= count <= size

        @pl.when(fits)
        def _():
            react(size)

        below = size


def home_kernel(in_ref, out_ref, rows_ref, sems):
    pieces, data, _ = in_ref.shape
    steps = sems.shape[0]
    part = data // steps
    copies = []
    for step in range(steps):
        size = part * pieces
        for y in range(pieces):
            at = pl.ds(step * size + y, part, stride=pieces)
            rows_ref[at, :] = in_ref[y, step * part : (step + 1) * part, :]
        at = pl.ds(step * size, size)
        copies.append(pltpu.make_async_copy(rows_ref.at[at], out_ref.at[at], sems.at[step]))
        copies[-1].start()
    for copy in copies:
        copy.wait()


def reaction_tables(stoich_ref, rates_ref, pairs_ref, partner_ref, squares_ref, produced_ref, species):
    rates = rates_ref[...]
    each = lax.broadcasted_iota(jnp.int32, (species, rates.shape[1]), 0)
    one, two, three, four = [jnp.where(each == stoich_ref[i : i + 1, :], 1.0, 0.0) for i in range(4)]
    both, produced = one + two, three + four
    along = (((1,), (1,)), ((), ()))
    highest = lax.Precision.HIGHEST
    scaled = rates * both
    partner = lax.dot_general(rates * one, two, along, highest, F32) + lax.dot_general(rates * two, one, along, highest, F32)
    squares = lax.dot_general(produced, 0.5 * scaled, along, highest, F32)
    pairs = jnp.sqrt(rates) * both
    high = pairs.astype(BF16).astype(F32)
    pairs_ref[...] = jnp.concatenate([high, high, pairs - high], 0).T.astype(BF16)
    partner_ref[...] = weights(partner)
    squares_ref[...] = weights(squares)
    half = (0.5 * produced).astype(BF16)
    produced_ref[...] = jnp.concatenate([half, half], 1)


def per_device(scalars, diffusivity, velocity, mixing, rates, stoich, burn_tile, helper_slot):
    block = lax.axis_index("space")
    blocks = lax.axis_size("space")
    fields = lax.axis_size("field")
    cells = scalars[0]
    species, planes, rows, width = cells.shape
    data = species * planes
    field = lax.axis_index("field")
    odd = block % 2
    late = (block % DEPTH) // (DEPTH // 2)
    near_plane = lax.dynamic_index_in_dim(cells, (1 - odd) * (planes - 1), 1, False)
    across_plane = lax.dynamic_index_in_dim(cells, odd * (planes - 1), 1, False)
    near_pairs = [(i, i ^ 1) for i in range(blocks)]
    half = [i % DEPTH < DEPTH // 2 for i in range(blocks)]
    across_pairs = [(i, (i + 1 if i % 2 else i - 1) % blocks) for i in range(blocks)]
    early_near = lax.ppermute(near_plane, "space", [p for p in near_pairs if half[p[0]]])
    across = lax.ppermute(across_plane, "space", across_pairs)
    late_near = lax.ppermute(near_plane, "space", [p for p in near_pairs if not half[p[0]]])
    received = [x.reshape(species * rows, width) for x in (early_near, across, late_near)]
    owned = sum(jnp.where(field == member, place, 0) for place, member in enumerate(ORDER))
    mixing_row = lax.dynamic_index_in_dim(mixing, owned, 1, False)
    reactions = rates.shape[0]
    pieces, *tables = pl.pallas_call(
        local_kernel,
        out_shape=(
            shape(rows, data + 8, width),
            jax.ShapeDtypeStruct((reactions, 3 * species), BF16),
            jax.ShapeDtypeStruct((species, 3 * species), BF16),
            jax.ShapeDtypeStruct((species, 3 * species), BF16),
            jax.ShapeDtypeStruct((species, 2 * reactions), BF16),
        ),
        in_specs=[SMEM] + [VMEM] * 6,
        out_specs=[VMEM] * 5,
        scratch_shapes=[pltpu.VMEM((data * rows, width), F32), pltpu.VMEM((planes * rows, width), F32)],
        compiler_params=LIMIT,
        name="local",
    )(block.reshape(1), cells, diffusivity, velocity, burn_tile[0], stoich, rates[None])
    pieces = pl.pallas_call(
        halo_kernel,
        out_shape=shape(rows, data + 8, width),
        in_specs=[SMEM] * 2 + [VMEM] * 6,
        out_specs=VMEM,
        input_output_aliases={2: 0},
        compiler_params=LIMIT,
        name="halo",
    )(odd.reshape(1), late.reshape(1), pieces, *received, diffusivity, velocity)
    pieces, tables, mixing_row = lax.optimization_barrier((pieces, tables, mixing_row))
    pieces = lax.all_to_all(pieces, "field", 0, 0, axis_index_groups=[list(ORDER)], tiled=True)
    pieces = pl.pallas_call(
        react_kernel,
        out_shape=shape(fields, data, width),
        in_specs=[VMEM] * 6,
        out_specs=VMEM,
        scratch_shapes=[pltpu.SMEM((fields * planes + 1,), jnp.int32)],
        compiler_params=LIMIT,
        name="react",
    )(pieces, mixing_row, *tables)
    pieces = lax.all_to_all(pieces, "field", 0, 0, axis_index_groups=[list(ORDER)], tiled=True)
    updated = pl.pallas_call(
        home_kernel,
        out_shape=shape(data * rows, width),
        in_specs=[VMEM],
        out_specs=pl.BlockSpec(memory_space=pltpu.HBM),
        scratch_shapes=[pltpu.VMEM((data * rows, width), F32), pltpu.SemaphoreType.DMA((8,))],
        compiler_params=LIMIT,
        name="home",
    )(pieces)
    return updated.reshape(1, species, planes, rows, width)


def solution(mesh):
    return jax.shard_map(
        per_device,
        mesh=mesh,
        in_specs=(
            P("field", None, "space", None, None),
            P("space", None, None),
            P("space", None, None),
            P("space", None, None),
            P(),
            P(),
            P("field", None, None),
            P("field", None, None),
        ),
        out_specs=P("field", None, "space", None, None),
        check_vma=False,
    )
```
